256 devices in a mesh: frame: 64 (over z_lo, y, x), row: 4 (over z_hi, core).
Axes of the slice: x: 4, y: 4, z: 8 (z_hi: 2, z_lo: 4; z = z_hi * 4 + z_lo), core: 2. Of those that a mesh axis runs over, the one named last changes fastest.
Arguments:
- clip: bfloat16 [128, 48, 128, 320], P('frame', 'row'), may hold values from -6 to 6
- w_spatial: bfloat16 [3, 3, 320, 320], replicated, may hold values from -0.109375 to 0.109375
- b_spatial: float32 [320], replicated, may hold values from -3 to 3
- w_temporal: bfloat16 [3, 320, 320], replicated, may hold values from -0.1875 to 0.1875
- b_temporal: float32 [320], replicated, may hold values from -3 to 3
- ln_gain: float32 [320], replicated, may hold values from 0.1 to 1.9
- ln_bias: float32 [320], replicated, may hold values from -3 to 3
- w_query: bfloat16 [320, 320], replicated, may hold values from -1.677051 to 1.677051
- w_key: bfloat16 [320, 320], replicated, may hold values from -1.677051 to 1.677051
- w_value: bfloat16 [320, 320], replicated, may hold values from -0.3125 to 0.3125
- w_out: bfloat16 [320, 320], replicated, may hold values from -0.3125 to 0.3125
- b_out: float32 [320], replicated, may hold values from -3 to 3
Outputs:
- mixed: bfloat16 [128, 48, 128, 320], P('frame', 'row')
The draws below stay inside these ranges and needn't reach their ends.
All inputs are finite; a program needn't handle non-finite values.
Results may differ from the reference program's by a relative error of at most 0.0062.
Values may be sent and summed in bfloat16 or wider, within the bound.
No kernel may reach another device: no remote copies, remote signals or barrier semaphores. Data moves between devices by JAX's collectives and lax.ppermute only.
A program may use at most 128 MiB of HBM per device.

```python
import jax
import jax.numpy as jnp
from jax import lax

C = 320
HEAD = 64
HEADS = 5
COLS = 128
FRAMES = 128
ROWS = 48


def shared_projection(key, salt):
    own = jax.random.normal(jax.random.fold_in(key, salt), (C, C), jnp.float32)
    values = own / jnp.sqrt(jnp.float32(C))
    limit = 30.0 / jnp.sqrt(jnp.float32(C))
    return jnp.clip(values, -limit, limit).astype(jnp.bfloat16)


def draw_w_query(key, part):
    return shared_projection(key, 1)


def draw_w_key(key, part):
    return shared_projection(key, 2)


def shard_levels(own_key, shape, pieces, low, largest):
    level, own = 1.0, jax.random.fold_in(own_key, 6)
    for axis_at, blocks in pieces:
        heights = jnp.exp(jax.random.uniform(jax.random.fold_in(own, axis_at), (blocks,), jnp.float32, low / len(pieces), largest / len(pieces)))
        level = level * jnp.repeat(heights, shape[axis_at] // blocks).reshape([-1 if axis == axis_at else 1 for axis in range(len(shape))])
    return level


def centred(rng, shape, scale, reach, split=(), kind=jnp.bfloat16):
    entries = jax.random.normal(rng, shape, jnp.float32) * scale
    if len(split) > 0:
        entries = shard_levels(rng, shape, split, -0.22, 0.18) * entries
    return jnp.clip(entries, min=-reach, max=reach).astype(kind)


def setup_inputs(seed: int = 0) -> dict:
    splits = jax.random.split(jax.random.key(seed), 13)
    clip = centred(splits[0], (FRAMES, ROWS, COLS, C), 1.0, 6.0, ((0, 64), (1, 4)))
    w_spatial = centred(splits[1], (3, 3, C, C), (9 * C) ** -0.5, 0.109375)
    b_spatial = centred(splits[2], (C,), 0.5, 3.0, (), jnp.float32)
    w_temporal = centred(splits[3], (3, C, C), (3 * C) ** -0.5, 0.1875)
    b_temporal = centred(splits[4], (C,), 0.5, 3.0, (), jnp.float32)
    ln_gain = jnp.clip(1.0 + 0.18 * jax.random.normal(splits[5], (C,), jnp.float32), 0.1, 1.9)
    ln_bias = centred(splits[6], (C,), 0.5, 3.0, (), jnp.float32)
    w_query = draw_w_query(jax.random.fold_in(splits[12], 71), 0)
    w_key = draw_w_key(jax.random.fold_in(splits[12], 71), 0)
    w_value = centred(splits[9], (C, C), C ** -0.5, 0.3125)
    w_out = centred(splits[10], (C, C), C ** -0.5, 0.3125)
    b_out = centred(splits[11], (C,), 0.5, 3.0, (), jnp.float32)
    return {"clip": clip, "w_spatial": w_spatial, "b_spatial": b_spatial, "w_temporal": w_temporal, "b_temporal": b_temporal, "ln_gain": ln_gain, "ln_bias": ln_bias, "w_query": w_query, "w_key": w_key, "w_value": w_value, "w_out": w_out, "b_out": b_out}


def spatial_frame(frame, w_spatial, b_spatial):
    rows = frame.shape[0]
    cols = frame.shape[1]
    padded = jnp.pad(frame.astype(jnp.float32), ((1, 1), (1, 1), (0, 0)))
    weights = w_spatial.astype(jnp.float32)
    total = jnp.zeros((rows, cols, weights.shape[3]), jnp.float32) + b_spatial
    for tap_row in range(3):
        for tap_col in range(3):
            window = padded[tap_row:tap_row + rows, tap_col:tap_col + cols]
            total = total + jnp.einsum('rwc,co->rwo', window, weights[tap_row, tap_col])
    return total.astype(jnp.bfloat16)

def temporal_column(column, w_temporal, b_temporal, ln_gain, ln_bias, w_query, w_key, w_value, w_out, b_out):
    frames = column.shape[0]
    padded = jnp.pad(column.astype(jnp.float32), ((1, 1), (0, 0), (0, 0)))
    kernel = w_temporal.astype(jnp.float32)
    total = column.astype(jnp.float32) + b_temporal
    for tap in range(3):
        total = total + jnp.einsum('fwc,co->fwo', padded[tap:tap + frames], kernel[tap])
    framed = total.astype(jnp.bfloat16)
    values32 = framed.astype(jnp.float32)
    center = lax.optimization_barrier(jnp.mean(values32, axis=-1, keepdims=True))
    spread = lax.optimization_barrier(jnp.mean((values32 - center) ** 2, axis=-1, keepdims=True))
    normed = ((values32 - center) / jnp.sqrt(spread + 1e-05) * ln_gain + ln_bias).astype(jnp.bfloat16)
    normed32 = normed.astype(jnp.float32)
    query = jnp.einsum('fwc,cd->fwd', normed32, w_query.astype(jnp.float32)).astype(jnp.bfloat16)
    key = jnp.einsum('fwc,cd->fwd', normed32, w_key.astype(jnp.float32)).astype(jnp.bfloat16)
    value = jnp.einsum('fwc,cd->fwd', normed32, w_value.astype(jnp.float32)).astype(jnp.bfloat16)
    cols = column.shape[1]
    query = query.astype(jnp.float32).reshape(frames, cols, HEADS, HEAD)
    key = key.astype(jnp.float32).reshape(frames, cols, HEADS, HEAD)
    value = value.astype(jnp.float32).reshape(frames, cols, HEADS, HEAD)
    scores = jnp.einsum('fwhd,gwhd->whfg', query, key) / jnp.sqrt(jnp.float32(HEAD))
    top = lax.optimization_barrier(jnp.max(scores, axis=-1, keepdims=True))
    raised = jnp.exp(scores - top)
    weights = (raised / lax.optimization_barrier(jnp.sum(raised, axis=-1, keepdims=True))).astype(jnp.bfloat16)
    attended = jnp.einsum('whfg,gwhd->fwhd', weights.astype(jnp.float32), value)
    attended = attended.reshape(frames, cols, HEADS * HEAD).astype(jnp.bfloat16)
    result = values32 + jnp.einsum('fwc,co->fwo', attended.astype(jnp.float32), w_out.astype(jnp.float32)) + b_out
    return result.astype(jnp.bfloat16)

def reference(clip, w_spatial, b_spatial, w_temporal, b_temporal, ln_gain, ln_bias, w_query, w_key, w_value, w_out, b_out):
    spatial = lax.map(lambda frame: spatial_frame(frame, w_spatial, b_spatial), clip)
    by_rows = jnp.moveaxis(spatial, 1, 0)
    mixed = lax.map(lambda column: temporal_column(column, w_temporal, b_temporal, ln_gain, ln_bias, w_query, w_key, w_value, w_out, b_out), by_rows)
    return jnp.moveaxis(mixed, 0, 1)
```

```python
import functools

import jax
import jax.numpy as jnp
from jax import lax
from jax.experimental import pallas as pl
from jax.experimental.pallas import tpu as pltpu
from jax.sharding import PartitionSpec as P


BF = jnp.bfloat16
F32 = jnp.float32
C = 320
CP = 384
LANES = 640
CHUNK = 4
GROUP = 8
UA = 4
UB = 1024
UC = 4
EXP_SCALE = 0.125 * 1.4426950408889634


def shift_rows(value, step):
    count = value.shape[0]
    turned = pltpu.roll(value, step % count, 0)
    row = lax.broadcasted_iota(jnp.int32, value.shape, 0)
    edge = 0 if step == 1 else count - 1
    return jnp.where(row == edge, 0.0, turned)


def conv_kernel(parts, rows, w_hbm, b_ref, x_hbm, low_hbm, high_hbm, out, *scratch):
    count = len(parts)
    strips, turned, w_ref, w_even, w_odd, x_sem, w_sem = scratch
    loads = []
    for h, chunk in enumerate(parts):
        first, last = chunk * CHUNK - 1, (chunk + 1) * CHUNK
        for f in range(2):
            pieces = [(x_hbm.at[f, max(first, 0) : min(last, rows - 1) + 1], int(first < 0))]
            if first < 0:
                pieces.append((low_hbm.at[f], 0))
            if last == rows:
                pieces.append((high_hbm.at[f], CHUNK + 1))
            for source, at in pieces:
                loads.append(
                    pltpu.make_async_copy(
                        source,
                        strips.at[h, f, at : at + source.shape[0]],
                        x_sem.at[len(loads)],
                    )
                )
    w_load = pltpu.make_async_copy(w_hbm, w_ref, w_sem)
    w_load.start()
    for load in loads:
        load.start()
    w_load.wait()
    w_even[960:1024, :] = jnp.zeros((64, 1024), BF)
    w_odd[0:64, :] = jnp.zeros((64, 1024), BF)
    for a in range(3):
        at = a * C
        for b in range(3):
            main = w_ref[a, b, :, 0:256]
            w_even[at : at + C, b * 256 : (b + 1) * 256] = main
            w_odd[64 + at : 64 + at + C, b * 256 : (b + 1) * 256] = main
        rest_w = jnp.concatenate(
            [w_ref[a, b, :, 256:C] for b in range(3)] + [jnp.zeros((C, 64), BF)], axis=1
        )
        w_even[at : at + C, 768:1024] = rest_w
        w_odd[64 + at : 64 + at + C, 768:1024] = rest_w
    for load in loads:
        load.wait()
    lane = lax.broadcasted_iota(jnp.int32, (128, 128), 1)
    for h in range(count):
        for f in range(2):
            turned[f] = strips[h, f].reshape((CHUNK + 2) * C, 128).T
        for odd, weights in ((0, w_even), (1, w_odd)):
            starts = (0, 640) if odd == 0 else (256, 896)
            left = jnp.concatenate(
                [turned[f, :, s : s + 1024] for s in starts for f in range(2)], axis=0
            )
            y = jnp.dot(left, weights[...], preferred_element_type=F32)
            for n in range(2):
                to = slice((odd + 2 * n) * 16, (odd + 2 * n + 1) * 16)
                tails = []
                for f in range(2):
                    at = (n * 2 + f) * 128
                    part = y[at : at + 128]
                    main = (
                        shift_rows(part[:, 0:256], 1)
                        + part[:, 256:512]
                        + shift_rows(part[:, 512:768], -1)
                        + b_ref[0:1, 0:256]
                    )
                    out[to, h, :, f * 256 : (f + 1) * 256] = main.reshape(16, 8, 256).astype(BF)
                    pair = part[:, 768:896]
                    tails.append(
                        shift_rows(pair, 1)
                        + pltpu.roll(pair, 64, 1)
                        + shift_rows(part[:, 896:1024], -1)
                        + b_ref[0:1, 256:384]
                    )
                tail = jnp.where(lane < 64, tails[0], pltpu.roll(tails[1], 64, 1))
                out[to, h, :, 512:640] = tail.reshape(16, 8, 128).astype(BF)


def spatial_chunk(parts, low, x, high, w, b):
    count = len(parts)
    rows = x.shape[1]
    shape = (64, count, 8, LANES)
    far = pl.BlockSpec(memory_space=pltpu.HBM)
    if parts[0] > 0:
        low = x
    if (parts[-1] + 1) * CHUNK < rows:
        high = x
    return pl.pallas_call(
        functools.partial(conv_kernel, parts, rows),
        out_shape=jax.ShapeDtypeStruct(shape, BF),
        grid=(1,),
        in_specs=[far, full((1, CP)), far, far, far],
        out_specs=full(shape),
        scratch_shapes=[
            pltpu.VMEM((count, 2, CHUNK + 2, C, 128), BF),
            pltpu.VMEM((2, 128, (CHUNK + 2) * C), BF),
            pltpu.VMEM((3, 3, C, C), BF),
            pltpu.VMEM((1024, 1024), BF),
            pltpu.VMEM((1024, 1024), BF),
            pltpu.SemaphoreType.DMA((4 * count,)),
            pltpu.SemaphoreType.DMA,
        ],
        compiler_params=pltpu.CompilerParams(vmem_limit_bytes=32 << 20),
        cost_estimate=pl.CostEstimate(
            flops=2200000000 * count, transcendentals=0, bytes_accessed=4000000 * count
        ),
        name="spatial",
    )(w, b, x, low, high)


def full(block):
    return pl.BlockSpec(block, lambda i: (0,) * len(block))


def attend_kernel(
    x_ref, we_hbm, wo_hbm, vector_ref, wqkv_hbm, wout_hbm, out_ref, *rest
):
    *rest, we_ref, wo_ref, wqkv_ref, wout_ref, sems = rest
    loads = [
        pltpu.make_async_copy(source, target, sems.at[n])
        for n, (source, target) in enumerate(
            ((we_hbm, we_ref), (wo_hbm, wo_ref), (wqkv_hbm, wqkv_ref), (wout_hbm, wout_ref))
        )
    ]

    @pl.when(pl.program_id(0) == 0)
    def _():
        for load in loads:
            load.start()

    bt_ref, gain_ref, bias_ref, bout_ref = (vector_ref.at[i : i + 1] for i in range(4))
    xs, le, lo, fe, fo, fr, nm, qkv, at, ys, sc, ex = rest
    xs[:, 0:8, :] = jnp.zeros((5, 8, 128), F32)
    xs[:, 520:528, :] = jnp.zeros((5, 8, 128), F32)
    for c in range(5):
        piece = x_ref[:, 0, :, c * 128 : (c + 1) * 128]
        xs[c, 8:520, :] = piece.astype(F32).reshape(512, 128)
    for p in range(GROUP):
        at_rows = slice(p * 64, (p + 1) * 64)
        for c in range(5):
            here = xs[c, pl.ds(8 + p, 64, stride=8), :].astype(BF)
            le[at_rows, 384 + c * 128 : 512 + c * 128] = here
            lo[at_rows, c * 128 : (c + 1) * 128] = here
        for n, c in enumerate((2, 3, 4)):
            before = xs[c, pl.ds(p, 64, stride=8), :].astype(BF)
            le[at_rows, n * 128 : (n + 1) * 128] = before
        for n, c in enumerate((0, 1, 4)):
            after = xs[c, pl.ds(16 + p, 64, stride=8), :].astype(BF)
            lo[at_rows, 640 + n * 128 : 768 + n * 128] = after

    @pl.when(pl.program_id(0) == 0)
    def _():
        for load in loads:
            load.wait()

    fe[...] = jnp.dot(le[...], we_ref[...], preferred_element_type=F32)
    fo[...] = jnp.dot(lo[...], wo_ref[...], preferred_element_type=F32)
    lane = lax.broadcasted_iota(jnp.int32, (64, 128), 1)
    keep = lane < 64

    def norm(p, carry):
        rows64 = pl.ds(pl.multiple_of(p * 64, 64), 64)
        tail = le[rows64, 896:1024].astype(F32)
        for odd, total in ((0, fe), (1, fo)):
            main = (
                total[rows64, 0:256]
                + le[rows64, 384 + 256 * odd : 640 + 256 * odd].astype(F32)
                + bt_ref[0:1, 0:256]
            )
            mine = pltpu.roll(tail, 64, 1) if odd else tail
            rim = total[rows64, 256:384] + jnp.where(keep, mine, 0.0) + bt_ref[0:1, 256:384]
            main = main.astype(BF)
            rim = rim.astype(BF)
            rows = pl.ds(pl.multiple_of(p * 128 + odd * 64, 64), 64)
            fr[rows, 0:256] = main
            fr[rows, 256:384] = rim
            main = main.astype(F32)
            rim = rim.astype(F32)
            mean = (
                jnp.sum(main[:, 0:128] + main[:, 128:256] + rim, axis=1, keepdims=True)
            ) * (1.0 / C)
            dm = main - mean
            dr = jnp.where(keep, rim - mean, 0.0)
            square = dm * dm
            var = jnp.sum(
                square[:, 0:128] + square[:, 128:256] + dr * dr, axis=1, keepdims=True
            ) * (1.0 / C)
            scale = lax.rsqrt(var + 1e-05)
            nm[rows, 0:256] = (
                dm * scale * gain_ref[0:1, 0:256] + bias_ref[0:1, 0:256]
            ).astype(BF)
            nm[rows, 256:384] = (
                dr * scale * gain_ref[0:1, 256:384] + bias_ref[0:1, 256:384]
            ).astype(BF)
        return carry

    lax.fori_loop(0, GROUP, norm, 0)
    for half in range(2):
        rows = slice(half * 512, (half + 1) * 512)
        qkv[rows, :] = jnp.dot(nm[rows, :], wqkv_ref[...], preferred_element_type=F32).astype(BF)

    wide = lax.broadcasted_iota(jnp.int32, (128, 128), 1) < 64

    nt = (((1,), (1,)), ((), ()))

    def score(step, carry):
        for u in range(UA):
            p = step * UA + u
            rows = pl.ds(pl.multiple_of(p * 128, 128), 128)
            for pair in range(2):
                q = qkv[rows, pair * 128 : (pair + 1) * 128]
                k = qkv[rows, 256 + pair * 128 : 384 + pair * 128]
                zero = jnp.zeros_like(q)
                both = jnp.concatenate(
                    [jnp.where(wide, q, zero), jnp.where(wide, zero, q)], axis=0
                )
                to = pl.ds(pl.multiple_of(p * 640 + pair * 256, 128), 256)
                sc[to, :] = lax.dot_general(both, k, nt, preferred_element_type=F32)
            to = pl.ds(pl.multiple_of(p * 640 + 512, 128), 128)
            sc[to, :] = lax.dot_general(
                qkv[rows, 768:896], qkv[rows, 896:1024], nt, preferred_element_type=F32
            )
        return carry

    lax.fori_loop(0, GROUP // UA, score, 0)

    def raise_all(step, carry):
        rows = pl.ds(pl.multiple_of(step * UB, UB), UB)
        scores = sc[rows, :]
        top = jnp.max(scores, axis=1, keepdims=True)
        ex[rows, :] = jnp.exp2((scores - top) * EXP_SCALE).astype(BF)
        return carry

    lax.fori_loop(0, GROUP * 640 // UB, raise_all, 0)
    ones = jnp.ones((128, 128), BF)

    def gather(step, carry):
        for u in range(UC):
            p = step * UC + u
            rows = pl.ds(pl.multiple_of(p * 128, 128), 128)
            for pair in range(2):
                v = qkv[rows, 512 + pair * 128 : 640 + pair * 128]
                to = pl.ds(pl.multiple_of(p * 640 + pair * 256, 128), 256)
                out = jnp.dot(
                    ex[to, :], jnp.concatenate([v, ones], axis=1), preferred_element_type=F32
                )
                top = jnp.where(wide, out[0:128, 0:128], out[128:256, 0:128])
                under = jnp.where(wide, out[0:128, 128:256], out[128:256, 128:256])
                at[rows, pair * 128 : (pair + 1) * 128] = (top / under).astype(BF)
            to = pl.ds(pl.multiple_of(p * 640 + 512, 128), 128)
            qv = qkv[rows, 768:896]
            out = jnp.dot(
                ex[to, :], jnp.concatenate([qv, ones], axis=1), preferred_element_type=F32
            )
            at[rows, 256:384] = (out[:, 0:128] / out[:, 128:256]).astype(BF)
        return carry

    lax.fori_loop(0, GROUP // UC, gather, 0)
    for half in range(2):
        rows = slice(half * 512, (half + 1) * 512)
        y = (
            fr[rows, :].astype(F32)
            + jnp.dot(at[rows, :], wout_ref[...], preferred_element_type=F32)
            + bout_ref[0:1, :]
        )
        for j in range(4):
            p = half * 4 + j
            even = y[j * 128 : j * 128 + 64]
            odd = y[j * 128 + 64 : j * 128 + 128]
            place = pl.ds(p, 64, stride=8)
            for c in range(2):
                ys[c, place, :] = even[:, c * 128 : (c + 1) * 128]
                ys[2 + c, place, :] = odd[:, c * 128 : (c + 1) * 128]
            ys[4, place, :] = jnp.where(keep, even[:, 256:384], pltpu.roll(odd[:, 256:384], 64, 1))
    for c in range(5):
        piece = ys[c].reshape(64, 8, 128)
        out_ref[:, 0, :, c * 128 : (c + 1) * 128] = piece.astype(BF)


def attend_chunk(x, weights):
    count = x.shape[1]
    block = pl.BlockSpec((64, 1, 8, LANES), lambda i: (0, i, 0, 0))
    far = pl.BlockSpec(memory_space=pltpu.HBM)
    return pl.pallas_call(
        attend_kernel,
        out_shape=jax.ShapeDtypeStruct(x.shape, BF),
        grid=(count,),
        in_specs=[block, far, far, full(weights[2].shape), far, far],
        out_specs=block,
        scratch_shapes=[
            pltpu.VMEM((5, 528, 128), F32),
            pltpu.VMEM((512, 1024), BF),
            pltpu.VMEM((512, 1024), BF),
            pltpu.VMEM((512, CP), F32),
            pltpu.VMEM((512, CP), F32),
            pltpu.VMEM((1024, CP), BF),
            pltpu.VMEM((1024, CP), BF),
            pltpu.VMEM((1024, 1024), BF),
            pltpu.VMEM((1024, CP), BF),
            pltpu.VMEM((5, 512, 128), F32),
            pltpu.VMEM((5120, 128), F32),
            pltpu.VMEM((5120, 128), BF),
            pltpu.VMEM((1024, CP), BF),
            pltpu.VMEM((1024, CP), BF),
            pltpu.VMEM((CP, 1024), BF),
            pltpu.VMEM((CP, CP), BF),
            pltpu.SemaphoreType.DMA((4,)),
        ],
        compiler_params=pltpu.CompilerParams(vmem_limit_bytes=32 << 20),
        cost_estimate=pl.CostEstimate(
            flops=4000000000 * count, transcendentals=700000 * count, bytes_accessed=4000000 * count
        ),
        name="attend",
    )(x, *weights)


def final_kernel(x_ref, *rest):
    out = rest[-1]
    for i in range(CHUNK):
        y = x_ref[i * 16 : (i + 1) * 16, 0].reshape(128, LANES).T
        out[0, i, 0:256, :] = y[0:256]
        out[1, i, 0:256, :] = y[256:512]
        out[0, i, 256:320, :] = y[512:576]
        out[1, i, 256:320, :] = y[576:640]


def final_chunk(x, held, first, step, rows):
    count = x.shape[1]
    operands = [x]
    specs = [pl.BlockSpec((64, 1, 8, LANES), lambda i: (0, i, 0, 0))]
    aliases = {}
    if held is not None:
        operands.append(held)
        specs.append(pl.BlockSpec(memory_space=pl.ANY))
        aliases = {1: 0}
    return pl.pallas_call(
        final_kernel,
        out_shape=jax.ShapeDtypeStruct((2, rows, C, 128), BF),
        grid=(count,),
        in_specs=specs,
        out_specs=pl.BlockSpec((2, CHUNK, C, 128), lambda i: (0, first + i * step, 0, 0)),
        input_output_aliases=aliases,
        compiler_params=pltpu.CompilerParams(vmem_limit_bytes=16 << 20),
        cost_estimate=pl.CostEstimate(
            flops=0, transcendentals=0, bytes_accessed=1400000 * count
        ),
        name="final",
    )(*operands)


def widened(vector):
    return jnp.pad(vector, (0, CP - C)).reshape(1, CP)


def prepare_kernel(wt_ref, wq_ref, wk_ref, wv_ref, wo_ref, *outs):
    even, odd, qkv, mix = outs
    zero = jnp.zeros((64, CP), BF)
    side = jnp.zeros((C, 64), BF)
    wide = [jnp.concatenate([wt_ref[k], side], axis=1) for k in range(3)]
    a, b, c = 256, 320, 384
    for at, tap, low, high in (
        (0, 0, 0, a),
        (c - 64, 0, a, b),
        (c, 1, 0, a),
        (640, 2, 0, a),
        (896, 1, a, b),
        (960, 2, a, b),
    ):
        even[at : at + high - low, :] = wide[tap][low:high]
    even[a:b, :] = zero
    for at, tap, low, high in (
        (0, 0, 0, a),
        (a, 1, 0, a),
        (512, 0, a, b),
        (576, 1, a, b),
        (640, 2, 0, a),
        (896, 2, a, b),
    ):
        odd[at : at + high - low, :] = wide[tap][low:high]
    odd[960:1024, :] = zero
    qkv[C:CP, :] = jnp.zeros((64, 1024), BF)
    qkv[0:C, 0:256] = wq_ref[:, 0:256]
    qkv[0:C, 256:512] = wk_ref[:, 0:256]
    qkv[0:C, 512:768] = wv_ref[:, 0:256]
    qkv[0:C, 768:896] = jnp.concatenate([wq_ref[:, 256:C], wv_ref[:, 256:C]], axis=1)
    qkv[0:C, 896:1024] = jnp.concatenate([wk_ref[:, 256:C], side], axis=1)
    out = jnp.concatenate([wo_ref[...], side], axis=1)
    mix[0:256, :] = out[0:256]
    mix[256:320, :] = zero
    mix[320:384, :] = out[256:320]


def prepared(w_temporal, w_query, w_key, w_value, w_out):
    square = full((C, C))
    shapes = ((1024, CP), (1024, CP), (CP, 1024), (CP, CP))
    return pl.pallas_call(
        prepare_kernel,
        out_shape=[pltpu.HBM(shape, BF) for shape in shapes],
        grid=(1,),
        in_specs=[full((3, C, C)), square, square, square, square],
        out_specs=[full(shape) for shape in shapes],
        compiler_params=pltpu.CompilerParams(vmem_limit_bytes=16 << 20),
        cost_estimate=pl.CostEstimate(flops=0, transcendentals=0, bytes_accessed=5000000),
        name="prepare",
    )(w_temporal, w_query, w_key, w_value, w_out)


def on_device(
    clip,
    w_spatial,
    b_spatial,
    w_temporal,
    b_temporal,
    ln_gain,
    ln_bias,
    w_query,
    w_key,
    w_value,
    w_out,
    b_out,
):
    rows = clip.shape[1]
    x = jnp.transpose(clip, (0, 1, 3, 2))
    row_count = lax.axis_size("row")
    forward = [(i, i + 1) for i in range(row_count - 1)]
    backward = [(b, a) for a, b in forward]
    low = lax.ppermute(x[:, rows - 1 :], "row", forward)
    high = lax.ppermute(x[:, :1], "row", backward)
    x = pltpu.with_memory_space_constraint(x, pltpu.HBM)
    w_spatial = pltpu.with_memory_space_constraint(w_spatial, pltpu.HBM)
    bias = widened(b_spatial)
    w_even, w_odd, w_qkv, w_mix = prepared(w_temporal, w_query, w_key, w_value, w_out)
    vectors = jnp.pad(jnp.stack([b_temporal, ln_gain, ln_bias, b_out]), ((0, 4), (0, CP - C)))
    w_even, w_odd, w_qkv, w_mix = (
        pltpu.with_memory_space_constraint(w, pltpu.HBM) for w in (w_even, w_odd, w_qkv, w_mix)
    )
    weights = (w_even, w_odd, vectors, w_qkv, w_mix)

    def exchange(value):
        return lax.all_to_all(value, "frame", split_axis=0, concat_axis=0, tiled=True)

    held = None
    for parts in ((1,), (0, 2)):
        sent = spatial_chunk(parts, low, x, high, w_spatial, bias)
        sent = exchange(sent)
        sent = attend_chunk(sent, weights)
        sent = exchange(sent)
        held = final_chunk(sent, held, parts[0], parts[-1] - parts[0], rows)
    return jnp.transpose(held, (0, 1, 3, 2))


def solution(mesh):
    placed = (P("frame", "row", None, None),) + (P(),) * 11
    return jax.shard_map(
        on_device,
        mesh=mesh,
        in_specs=placed,
        out_specs=P("frame", "row", None, None),
        check_vma=False,
    )
```

```python
import functools

import jax
import jax.numpy as jnp
from jax import lax
from jax.experimental import pallas as pl
from jax.experimental.pallas import tpu as pltpu
from jax.sharding import PartitionSpec as P


BF = jnp.bfloat16
F32 = jnp.float32
C = 320
CP = 384
LANES = 640
CHUNK = 4
GROUP = 8
ORDER = (
    22, 12, 52, 3, 19, 5, 60, 58, 2, 33, 10, 8, 29, 26, 25, 9,
    44, 18, 62, 11, 47, 40, 15, 39, 56, 57, 32, 23, 49, 43, 21, 45,
    42, 34, 35, 46, 20, 61, 37, 14, 63, 53, 0, 38, 27, 50, 1, 55,
    6, 13, 24, 41, 30, 28, 59, 31, 7, 16, 4, 48, 51, 54, 36, 17,
)
EXP_SCALE = 0.125 * 1.4426950408889634


def shift_rows(value, step):
    count = value.shape[0]
    turned = pltpu.roll(value, step % count, 0)
    row = lax.broadcasted_iota(jnp.int32, value.shape, 0)
    edge = 0 if step == 1 else count - 1
    return jnp.where(row == edge, 0.0, turned)


def conv_kernel(parts, rows, w_hbm, b_ref, x_hbm, low_hbm, high_hbm, out, *scratch):
    count = len(parts)
    strips, turned, w_ref, w_even, w_odd, x_sem, w_sem = scratch
    loads = []
    for h, chunk in enumerate(parts):
        first, last = chunk * CHUNK - 1, (chunk + 1) * CHUNK
        for f in range(2):
            pieces = [(x_hbm.at[f, max(first, 0) : min(last, rows - 1) + 1], int(first < 0))]
            if first < 0:
                pieces.append((low_hbm.at[f], 0))
            if last == rows:
                pieces.append((high_hbm.at[f], CHUNK + 1))
            for source, at in pieces:
                loads.append(
                    pltpu.make_async_copy(
                        source,
                        strips.at[h, f, at : at + source.shape[0]],
                        x_sem.at[len(loads)],
                    )
                )
    w_loads = [pltpu.make_async_copy(w_hbm.at[a], w_ref.at[a], w_sem.at[a]) for a in range(3)]
    for load in loads + w_loads:
        load.start()
    for load in loads:
        load.wait()
    for h in range(count):
        for f in range(2):
            turned[h, f] = strips[h, f].reshape((CHUNK + 2) * C, 128).T
    w_even[960:1024, :] = jnp.zeros((64, 1024), BF)
    w_odd[0:64, :] = jnp.zeros((64, 1024), BF)
    for a in range(3):
        w_loads[a].wait()
        at = a * C
        for b in range(3):
            main = w_ref[a, b, :, 0:256]
            w_even[at : at + C, b * 256 : (b + 1) * 256] = main
            w_odd[64 + at : 64 + at + C, b * 256 : (b + 1) * 256] = main
        rest_w = jnp.concatenate(
            [w_ref[a, b, :, 256:C] for b in range(3)] + [jnp.zeros((C, 64), BF)], axis=1
        )
        w_even[at : at + C, 768:1024] = rest_w
        w_odd[64 + at : 64 + at + C, 768:1024] = rest_w
    lane = lax.broadcasted_iota(jnp.int32, (128, 128), 1)
    for h in range(count):
        for odd, weights in ((0, w_even), (1, w_odd)):
            starts = (0, 640) if odd == 0 else (256, 896)
            left = jnp.concatenate(
                [turned[h, f, :, s : s + 1024] for s in starts for f in range(2)], axis=0
            )
            y = jnp.dot(left, weights[...], preferred_element_type=F32)
            for n in range(2):
                to = slice((odd + 2 * n) * 16, (odd + 2 * n + 1) * 16)
                tails = []
                for f in range(2):
                    at = (n * 2 + f) * 128
                    part = y[at : at + 128]
                    main = (
                        shift_rows(part[:, 0:256], 1)
                        + part[:, 256:512]
                        + shift_rows(part[:, 512:768], -1)
                        + b_ref[0:1, 0:256]
                    )
                    out[to, h, :, f * 256 : (f + 1) * 256] = main.reshape(16, 8, 256).astype(BF)
                    pair = part[:, 768:896]
                    tails.append(
                        shift_rows(pair, 1)
                        + pltpu.roll(pair, 64, 1)
                        + shift_rows(part[:, 896:1024], -1)
                        + b_ref[0:1, 256:384]
                    )
                tail = jnp.where(lane < 64, tails[0], pltpu.roll(tails[1], 64, 1))
                out[to, h, :, 512:640] = tail.reshape(16, 8, 128).astype(BF)


def spatial_chunk(parts, low, x, high, w, b):
    count = len(parts)
    rows = x.shape[1]
    shape = (64, count, 8, LANES)
    far = pl.BlockSpec(memory_space=pltpu.HBM)
    if parts[0] > 0:
        low = x
    if (parts[-1] + 1) * CHUNK < rows:
        high = x
    return pl.pallas_call(
        functools.partial(conv_kernel, parts, rows),
        out_shape=jax.ShapeDtypeStruct(shape, BF),
        grid=(1,),
        in_specs=[far, full((1, CP)), far, far, far],
        out_specs=full(shape),
        scratch_shapes=[
            pltpu.VMEM((count, 2, CHUNK + 2, C, 128), BF),
            pltpu.VMEM((count, 2, 128, (CHUNK + 2) * C), BF),
            pltpu.VMEM((3, 3, C, C), BF),
            pltpu.VMEM((1024, 1024), BF),
            pltpu.VMEM((1024, 1024), BF),
            pltpu.SemaphoreType.DMA((4 * count,)),
            pltpu.SemaphoreType.DMA((3,)),
        ],
        compiler_params=pltpu.CompilerParams(vmem_limit_bytes=32 << 20),
        cost_estimate=pl.CostEstimate(
            flops=2200000000 * count, transcendentals=0, bytes_accessed=4000000 * count
        ),
        name="spatial",
    )(w, b, x, low, high)


def full(block):
    return pl.BlockSpec(block, lambda i: (0,) * len(block))


def attend_kernel(
    x_ref, we_hbm, wo_hbm, vector_ref, wqkv_hbm, wout_hbm, out_ref, *rest
):
    *rest, we_ref, wo_ref, wqkv_ref, wout_ref, sems = rest
    loads = [
        pltpu.make_async_copy(source, target, sems.at[n])
        for n, (source, target) in enumerate(
            ((we_hbm, we_ref), (wo_hbm, wo_ref), (wqkv_hbm, wqkv_ref), (wout_hbm, wout_ref))
        )
    ]

    @pl.when(pl.program_id(0) == 0)
    def _():
        for load in loads:
            load.start()

    bt_ref, gain_ref, bias_ref, bout_ref = (vector_ref.at[i : i + 1] for i in range(4))
    xs, le, lo, fe, fo, fr, nm, qkv, at, ys, sc, ex = rest
    xs[:, 0:8, :] = jnp.zeros((5, 8, 128), F32)
    xs[:, 520:528, :] = jnp.zeros((5, 8, 128), F32)
    for c in range(5):
        lanes = slice(c * 128, (c + 1) * 128)
        for j, pair in enumerate(ORDER):
            xs[c, 8 + pair * 8 : 16 + pair * 8, :] = x_ref[j, 0, :, lanes].astype(F32)
    for p in range(GROUP):
        at_rows = slice(p * 64, (p + 1) * 64)
        for c in range(5):
            here = xs[c, pl.ds(8 + p, 64, stride=8), :].astype(BF)
            le[at_rows, 384 + c * 128 : 512 + c * 128] = here
            lo[at_rows, c * 128 : (c + 1) * 128] = here
        for n, c in enumerate((2, 3, 4)):
            before = xs[c, pl.ds(p, 64, stride=8), :].astype(BF)
            le[at_rows, n * 128 : (n + 1) * 128] = before
        for n, c in enumerate((0, 1, 4)):
            after = xs[c, pl.ds(16 + p, 64, stride=8), :].astype(BF)
            lo[at_rows, 640 + n * 128 : 768 + n * 128] = after

    @pl.when(pl.program_id(0) == 0)
    def _():
        for load in loads:
            load.wait()

    fe[...] = jnp.dot(le[...], we_ref[...], preferred_element_type=F32)
    fo[...] = jnp.dot(lo[...], wo_ref[...], preferred_element_type=F32)
    lane = lax.broadcasted_iota(jnp.int32, (64, 128), 1)
    keep = lane < 64

    def norm(p, carry):
        rows64 = pl.ds(pl.multiple_of(p * 64, 64), 64)
        tail = le[rows64, 896:1024].astype(F32)
        for odd, total in ((0, fe), (1, fo)):
            main = (
                total[rows64, 0:256]
                + le[rows64, 384 + 256 * odd : 640 + 256 * odd].astype(F32)
                + bt_ref[0:1, 0:256]
            )
            mine = pltpu.roll(tail, 64, 1) if odd else tail
            rim = total[rows64, 256:384] + jnp.where(keep, mine, 0.0) + bt_ref[0:1, 256:384]
            main = main.astype(BF)
            rim = rim.astype(BF)
            rows = pl.ds(pl.multiple_of(p * 128 + odd * 64, 64), 64)
            fr[rows, 0:256] = main
            fr[rows, 256:384] = rim
            main = main.astype(F32)
            rim = rim.astype(F32)
            mean = (
                jnp.sum(main[:, 0:128] + main[:, 128:256] + rim, axis=1, keepdims=True)
            ) * (1.0 / C)
            dm = main - mean
            dr = jnp.where(keep, rim - mean, 0.0)
            square = dm * dm
            var = jnp.sum(
                square[:, 0:128] + square[:, 128:256] + dr * dr, axis=1, keepdims=True
            ) * (1.0 / C)
            scale = lax.rsqrt(var + 1e-05)
            nm[rows, 0:256] = (
                dm * scale * gain_ref[0:1, 0:256] + bias_ref[0:1, 0:256]
            ).astype(BF)
            nm[rows, 256:384] = (
                dr * scale * gain_ref[0:1, 256:384] + bias_ref[0:1, 256:384]
            ).astype(BF)
        return carry

    lax.fori_loop(0, GROUP, norm, 0)
    for half in range(2):
        rows = slice(half * 512, (half + 1) * 512)
        qkv[rows, :] = jnp.dot(nm[rows, :], wqkv_ref[...], preferred_element_type=F32).astype(BF)

    wide = lax.broadcasted_iota(jnp.int32, (128, 128), 1) < 64

    nt = (((1,), (1,)), ((), ()))

    ones = jnp.ones((128, 128), BF)

    def score(p):
        rows = pl.ds(pl.multiple_of(p * 128, 128), 128)
        for pair in range(2):
            q = qkv[rows, pair * 128 : (pair + 1) * 128]
            k = qkv[rows, 256 + pair * 128 : 384 + pair * 128]
            zero = jnp.zeros_like(q)
            both = jnp.concatenate([jnp.where(wide, q, zero), jnp.where(wide, zero, q)], axis=0)
            to = pl.ds(pl.multiple_of(p * 640 + pair * 256, 128), 256)
            sc[to, :] = lax.dot_general(both, k, nt, preferred_element_type=F32)
        to = pl.ds(pl.multiple_of(p * 640 + 512, 128), 128)
        sc[to, :] = lax.dot_general(
            qkv[rows, 768:896], qkv[rows, 896:1024], nt, preferred_element_type=F32
        )

    def raise_one(p):
        for at5 in range(5):
            rows = pl.ds(pl.multiple_of(p * 640 + at5 * 128, 128), 128)
            scores = sc[rows, :]
            top = jnp.max(scores, axis=1, keepdims=True)
            ex[rows, :] = jnp.exp2((scores - top) * EXP_SCALE).astype(BF)

    def gather(p):
        rows = pl.ds(pl.multiple_of(p * 128, 128), 128)
        for pair in range(2):
            v = qkv[rows, 512 + pair * 128 : 640 + pair * 128]
            to = pl.ds(pl.multiple_of(p * 640 + pair * 256, 128), 256)
            out = jnp.dot(
                ex[to, :], jnp.concatenate([v, ones], axis=1), preferred_element_type=F32
            )
            top = jnp.where(wide, out[0:128, 0:128], out[128:256, 0:128])
            under = jnp.where(wide, out[0:128, 128:256], out[128:256, 128:256])
            at[rows, pair * 128 : (pair + 1) * 128] = (top / under).astype(BF)
        to = pl.ds(pl.multiple_of(p * 640 + 512, 128), 128)
        qv = qkv[rows, 768:896]
        out = jnp.dot(ex[to, :], jnp.concatenate([qv, ones], axis=1), preferred_element_type=F32)
        at[rows, 256:384] = (out[:, 0:128] / out[:, 128:256]).astype(BF)

    def step(p, carry):
        gather(p - 2)
        raise_one(p - 1)
        score(p)
        return carry

    score(0)
    raise_one(0)
    score(1)
    lax.fori_loop(2, GROUP, step, 0)
    gather(GROUP - 2)
    raise_one(GROUP - 1)
    gather(GROUP - 1)
    for half in range(2):
        rows = slice(half * 512, (half + 1) * 512)
        y = (
            fr[rows, :].astype(F32)
            + jnp.dot(at[rows, :], wout_ref[...], preferred_element_type=F32)
            + bout_ref[0:1, :]
        )
        for j in range(4):
            p = half * 4 + j
            even = y[j * 128 : j * 128 + 64]
            odd = y[j * 128 + 64 : j * 128 + 128]
            place = pl.ds(p, 64, stride=8)
            for c in range(2):
                ys[c, place, :] = even[:, c * 128 : (c + 1) * 128]
                ys[2 + c, place, :] = odd[:, c * 128 : (c + 1) * 128]
            ys[4, place, :] = jnp.where(keep, even[:, 256:384], pltpu.roll(odd[:, 256:384], 64, 1))
    for c in range(5):
        lanes = slice(c * 128, (c + 1) * 128)
        for j, pair in enumerate(ORDER):
            out_ref[j, 0, :, lanes] = ys[c, pair * 8 : pair * 8 + 8, :].astype(BF)


def attend_chunk(x, weights):
    count = x.shape[1]
    block = pl.BlockSpec((64, 1, 8, LANES), lambda i: (0, i, 0, 0))
    far = pl.BlockSpec(memory_space=pltpu.HBM)
    return pl.pallas_call(
        attend_kernel,
        out_shape=jax.ShapeDtypeStruct(x.shape, BF),
        grid=(count,),
        in_specs=[block, far, far, full(weights[2].shape), far, far],
        out_specs=block,
        scratch_shapes=[
            pltpu.VMEM((5, 528, 128), F32),
            pltpu.VMEM((512, 1024), BF),
            pltpu.VMEM((512, 1024), BF),
            pltpu.VMEM((512, CP), F32),
            pltpu.VMEM((512, CP), F32),
            pltpu.VMEM((1024, CP), BF),
            pltpu.VMEM((1024, CP), BF),
            pltpu.VMEM((1024, 1024), BF),
            pltpu.VMEM((1024, CP), BF),
            pltpu.VMEM((5, 512, 128), F32),
            pltpu.VMEM((5120, 128), F32),
            pltpu.VMEM((5120, 128), BF),
            pltpu.VMEM((1024, CP), BF),
            pltpu.VMEM((1024, CP), BF),
            pltpu.VMEM((CP, 1024), BF),
            pltpu.VMEM((CP, CP), BF),
            pltpu.SemaphoreType.DMA((4,)),
        ],
        compiler_params=pltpu.CompilerParams(vmem_limit_bytes=32 << 20),
        cost_estimate=pl.CostEstimate(
            flops=4000000000 * count, transcendentals=700000 * count, bytes_accessed=4000000 * count
        ),
        name="attend",
    )(x, *weights)


def final_kernel(x_ref, *rest):
    out = rest[-1]
    for i in range(CHUNK):
        y = x_ref[i * 16 : (i + 1) * 16, 0].reshape(128, LANES).T
        out[0, i, 0:256, :] = y[0:256]
        out[1, i, 0:256, :] = y[256:512]
        out[0, i, 256:320, :] = y[512:576]
        out[1, i, 256:320, :] = y[576:640]


def final_chunk(x, held, first, step, rows):
    count = x.shape[1]
    operands = [x]
    specs = [pl.BlockSpec((64, 1, 8, LANES), lambda i: (0, i, 0, 0))]
    aliases = {}
    if held is not None:
        operands.append(held)
        specs.append(pl.BlockSpec(memory_space=pl.ANY))
        aliases = {1: 0}
    return pl.pallas_call(
        final_kernel,
        out_shape=jax.ShapeDtypeStruct((2, rows, C, 128), BF),
        grid=(count,),
        in_specs=specs,
        out_specs=pl.BlockSpec((2, CHUNK, C, 128), lambda i: (0, first + i * step, 0, 0)),
        input_output_aliases=aliases,
        compiler_params=pltpu.CompilerParams(vmem_limit_bytes=16 << 20),
        cost_estimate=pl.CostEstimate(
            flops=0, transcendentals=0, bytes_accessed=1400000 * count
        ),
        name="final",
    )(*operands)


def widened(vector):
    return jnp.pad(vector, (0, CP - C)).reshape(1, CP)


def prepare_kernel(wt_ref, wq_ref, wk_ref, wv_ref, wo_ref, *outs):
    even, odd, qkv, mix = outs
    zero = jnp.zeros((64, CP), BF)
    side = jnp.zeros((C, 64), BF)
    wide = [jnp.concatenate([wt_ref[k], side], axis=1) for k in range(3)]
    a, b, c = 256, 320, 384
    for at, tap, low, high in (
        (0, 0, 0, a),
        (c - 64, 0, a, b),
        (c, 1, 0, a),
        (640, 2, 0, a),
        (896, 1, a, b),
        (960, 2, a, b),
    ):
        even[at : at + high - low, :] = wide[tap][low:high]
    even[a:b, :] = zero
    for at, tap, low, high in (
        (0, 0, 0, a),
        (a, 1, 0, a),
        (512, 0, a, b),
        (576, 1, a, b),
        (640, 2, 0, a),
        (896, 2, a, b),
    ):
        odd[at : at + high - low, :] = wide[tap][low:high]
    odd[960:1024, :] = zero
    qkv[C:CP, :] = jnp.zeros((64, 1024), BF)
    qkv[0:C, 0:256] = wq_ref[:, 0:256]
    qkv[0:C, 256:512] = wk_ref[:, 0:256]
    qkv[0:C, 512:768] = wv_ref[:, 0:256]
    qkv[0:C, 768:896] = jnp.concatenate([wq_ref[:, 256:C], wv_ref[:, 256:C]], axis=1)
    qkv[0:C, 896:1024] = jnp.concatenate([wk_ref[:, 256:C], side], axis=1)
    out = jnp.concatenate([wo_ref[...], side], axis=1)
    mix[0:256, :] = out[0:256]
    mix[256:320, :] = zero
    mix[320:384, :] = out[256:320]


def prepared(w_temporal, w_query, w_key, w_value, w_out):
    square = full((C, C))
    shapes = ((1024, CP), (1024, CP), (CP, 1024), (CP, CP))
    return pl.pallas_call(
        prepare_kernel,
        out_shape=[pltpu.HBM(shape, BF) for shape in shapes],
        grid=(1,),
        in_specs=[full((3, C, C)), square, square, square, square],
        out_specs=[full(shape) for shape in shapes],
        compiler_params=pltpu.CompilerParams(vmem_limit_bytes=16 << 20),
        cost_estimate=pl.CostEstimate(flops=0, transcendentals=0, bytes_accessed=5000000),
        name="prepare",
    )(w_temporal, w_query, w_key, w_value, w_out)


def on_device(
    clip,
    w_spatial,
    b_spatial,
    w_temporal,
    b_temporal,
    ln_gain,
    ln_bias,
    w_query,
    w_key,
    w_value,
    w_out,
    b_out,
):
    rows = clip.shape[1]
    x = jnp.transpose(clip, (0, 1, 3, 2))
    row_count = lax.axis_size("row")
    forward = [(i, i + 1) for i in range(row_count - 1)]
    backward = [(b, a) for a, b in forward]
    low = lax.ppermute(x[:, rows - 1 :], "row", forward)
    high = lax.ppermute(x[:, :1], "row", backward)
    x = pltpu.with_memory_space_constraint(x, pltpu.HBM)
    w_spatial = pltpu.with_memory_space_constraint(w_spatial, pltpu.HBM)
    bias = widened(b_spatial)
    w_even, w_odd, w_qkv, w_mix = prepared(w_temporal, w_query, w_key, w_value, w_out)
    vectors = jnp.pad(jnp.stack([b_temporal, ln_gain, ln_bias, b_out]), ((0, 4), (0, CP - C)))
    w_even, w_odd, w_qkv, w_mix = (
        pltpu.with_memory_space_constraint(w, pltpu.HBM) for w in (w_even, w_odd, w_qkv, w_mix)
    )
    weights = (w_even, w_odd, vectors, w_qkv, w_mix)

    def exchange(value):
        return lax.all_to_all(
            value,
            "frame",
            split_axis=0,
            concat_axis=0,
            tiled=True,
            axis_index_groups=[list(ORDER)],
        )

    held = None
    for parts in ((1,), (0, 2)):
        sent = spatial_chunk(parts, low, x, high, w_spatial, bias)
        sent = exchange(sent)
        sent = attend_chunk(sent, weights)
        sent = exchange(sent)
        held = final_chunk(sent, held, parts[0], parts[-1] - parts[0], rows)
    return jnp.transpose(held, (0, 1, 3, 2))


def solution(mesh):
    placed = (P("frame", "row", None, None),) + (P(),) * 11
    return jax.shard_map(
        on_device,
        mesh=mesh,
        in_specs=placed,
        out_specs=P("frame", "row", None, None),
        check_vma=False,
    )
```

```python
import functools

import jax
import jax.numpy as jnp
from jax import lax
from jax.experimental import pallas as pl
from jax.experimental.pallas import tpu as pltpu
from jax.sharding import PartitionSpec as P


BF = jnp.bfloat16
F32 = jnp.float32
C = 320
CP = 384
LANES = 640
CHUNK = 4
GROUP = 8
NORM_UNROLL = 2
ORDER = (
    22, 12, 52, 3, 19, 5, 60, 58, 2, 33, 10, 8, 29, 26, 25, 9,
    44, 18, 62, 11, 47, 40, 15, 39, 56, 57, 32, 23, 49, 43, 21, 45,
    42, 34, 35, 46, 20, 61, 37, 14, 63, 53, 0, 38, 27, 50, 1, 55,
    6, 13, 24, 41, 30, 28, 59, 31, 7, 16, 4, 48, 51, 54, 36, 17,
)
EXP_SCALE = 0.125 * 1.4426950408889634


def shift_rows(value, step):
    count = value.shape[0]
    turned = pltpu.roll(value, step % count, 0)
    row = lax.broadcasted_iota(jnp.int32, value.shape, 0)
    edge = 0 if step == 1 else count - 1
    return jnp.where(row == edge, 0.0, turned)


def conv_kernel(parts, rows, w_hbm, b_ref, x_hbm, low_hbm, high_hbm, out, *scratch):
    count = len(parts)
    strips, turned, w_ref, w_even, w_odd, x_sem, w_sem = scratch
    loads = []
    for h, chunk in enumerate(parts):
        first, last = chunk * CHUNK - 1, (chunk + 1) * CHUNK
        for f in range(2):
            pieces = [(x_hbm.at[f, max(first, 0) : min(last, rows - 1) + 1], int(first < 0))]
            if first < 0:
                pieces.append((low_hbm.at[f], 0))
            if last == rows:
                pieces.append((high_hbm.at[f], CHUNK + 1))
            for source, at in pieces:
                loads.append(
                    pltpu.make_async_copy(
                        source,
                        strips.at[h, f, at : at + source.shape[0]],
                        x_sem.at[len(loads)],
                    )
                )
    w_loads = [pltpu.make_async_copy(w_hbm.at[a], w_ref.at[a], w_sem.at[a]) for a in range(3)]
    for load in loads + w_loads:
        load.start()
    for load in loads:
        load.wait()
    for h in range(count):
        for f in range(2):
            turned[h, f] = strips[h, f].reshape((CHUNK + 2) * C, 128).T
    w_even[960:1024, :] = jnp.zeros((64, 1024), BF)
    w_odd[0:64, :] = jnp.zeros((64, 1024), BF)
    for a in range(3):
        w_loads[a].wait()
        at = a * C
        for b in range(3):
            main = w_ref[a, b, :, 0:256]
            w_even[at : at + C, b * 256 : (b + 1) * 256] = main
            w_odd[64 + at : 64 + at + C, b * 256 : (b + 1) * 256] = main
        rest_w = jnp.concatenate(
            [w_ref[a, b, :, 256:C] for b in range(3)] + [jnp.zeros((C, 64), BF)], axis=1
        )
        w_even[at : at + C, 768:1024] = rest_w
        w_odd[64 + at : 64 + at + C, 768:1024] = rest_w
    lane = lax.broadcasted_iota(jnp.int32, (128, 128), 1)
    rim_bias = jnp.concatenate([b_ref[0:1, 256:C], jnp.zeros((1, 64), F32)], axis=1)
    for h in range(count):
        for odd, weights in ((0, w_even), (1, w_odd)):
            starts = (0, 640) if odd == 0 else (256, 896)
            left = jnp.concatenate(
                [turned[h, f, :, s : s + 1024] for s in starts for f in range(2)], axis=0
            )
            y = jnp.dot(left, weights[...], preferred_element_type=F32)
            for n in range(2):
                to = slice((odd + 2 * n) * 16, (odd + 2 * n + 1) * 16)
                tails = []
                for f in range(2):
                    at = (n * 2 + f) * 128
                    part = y[at : at + 128]
                    main = (
                        shift_rows(part[:, 0:256], 1)
                        + part[:, 256:512]
                        + shift_rows(part[:, 512:768], -1)
                        + b_ref[0:1, 0:256]
                    )
                    out[to, h, :, f * 256 : (f + 1) * 256] = main.reshape(16, 8, 256).astype(BF)
                    pair = part[:, 768:896]
                    tails.append(
                        shift_rows(pair, 1)
                        + pltpu.roll(pair, 64, 1)
                        + shift_rows(part[:, 896:1024], -1)
                        + rim_bias
                    )
                tail = jnp.where(lane < 64, tails[0], pltpu.roll(tails[1], 64, 1))
                out[to, h, :, 512:640] = tail.reshape(16, 8, 128).astype(BF)


def spatial_chunk(parts, low, x, high, w, b):
    count = len(parts)
    rows = x.shape[1]
    shape = (64, count, 8, LANES)
    far = pl.BlockSpec(memory_space=pltpu.HBM)
    if parts[0] > 0:
        low = x
    if (parts[-1] + 1) * CHUNK < rows:
        high = x
    return pl.pallas_call(
        functools.partial(conv_kernel, parts, rows),
        out_shape=jax.ShapeDtypeStruct(shape, BF),
        grid=(1,),
        in_specs=[far, full((1, C)), far, far, far],
        out_specs=full(shape),
        scratch_shapes=[
            pltpu.VMEM((count, 2, CHUNK + 2, C, 128), BF),
            pltpu.VMEM((count, 2, 128, (CHUNK + 2) * C), BF),
            pltpu.VMEM((3, 3, C, C), BF),
            pltpu.VMEM((1024, 1024), BF),
            pltpu.VMEM((1024, 1024), BF),
            pltpu.SemaphoreType.DMA((4 * count,)),
            pltpu.SemaphoreType.DMA((3,)),
        ],
        compiler_params=pltpu.CompilerParams(vmem_limit_bytes=32 << 20),
        cost_estimate=pl.CostEstimate(
            flops=2200000000 * count, transcendentals=0, bytes_accessed=4000000 * count
        ),
        name="spatial",
    )(w, b, x, low, high)


def full(block):
    return pl.BlockSpec(block, lambda i: (0,) * len(block))


def attend_kernel(
    x_ref, we_hbm, wo_hbm, vector_ref, wqkv_hbm, wout_hbm, out_ref, *rest
):
    *rest, we_ref, wo_ref, wqkv_ref, wout_ref, sems = rest
    loads = [
        pltpu.make_async_copy(source, target, sems.at[n])
        for n, (source, target) in enumerate(
            ((we_hbm, we_ref), (wo_hbm, wo_ref), (wqkv_hbm, wqkv_ref), (wout_hbm, wout_ref))
        )
    ]

    @pl.when(pl.program_id(0) == 0)
    def _():
        for load in loads:
            load.start()

    bt_ref, gain_ref, bias_ref, bout_ref = (vector_ref.at[i : i + 1] for i in range(4))
    xs, le, lo, fe, fo, fr, nm, qkv, at, ys, sc, ex = rest
    for c in range(5):
        lanes = slice(c * 128, (c + 1) * 128)
        for j in range(0, 64, 2):
            piece = x_ref[j : j + 2, 0, :, lanes].astype(F32)
            for n in range(2):
                to = ORDER[j + n] * 8
                xs[c, to : to + 8, :] = piece[n]
    for p in range(GROUP):
        at_rows = slice(p * 64, (p + 1) * 64)
        for c in range(5):
            here = xs[c, pl.ds(p, 64, stride=8), :]
            if c >= 2:
                before = shift_rows(here, 1).astype(BF)
                le[at_rows, (c - 2) * 128 : (c - 1) * 128] = before
            if c < 2 or c == 4:
                n = min(c, 2)
                after = shift_rows(here, -1).astype(BF)
                lo[at_rows, 640 + n * 128 : 768 + n * 128] = after
            here = here.astype(BF)
            le[at_rows, 384 + c * 128 : 512 + c * 128] = here
            lo[at_rows, c * 128 : (c + 1) * 128] = here

    @pl.when(pl.program_id(0) == 0)
    def _():
        for load in loads:
            load.wait()

    fe[...] = jnp.dot(le[...], we_ref[...], preferred_element_type=F32)
    fo[...] = jnp.dot(lo[...], wo_ref[...], preferred_element_type=F32)
    lane = lax.broadcasted_iota(jnp.int32, (64, 128), 1)
    keep = lane < 64

    def norm(p):
        rows64 = pl.ds(pl.multiple_of(p * 64, 64), 64)
        tail = le[rows64, 896:1024].astype(F32)
        for odd, total in ((0, fe), (1, fo)):
            main = (
                total[rows64, 0:256]
                + le[rows64, 384 + 256 * odd : 640 + 256 * odd].astype(F32)
                + bt_ref[0:1, 0:256]
            )
            mine = pltpu.roll(tail, 64, 1) if odd else tail
            rim = total[rows64, 256:384] + jnp.where(keep, mine, 0.0) + bt_ref[0:1, 256:384]
            main = main.astype(BF)
            rim = rim.astype(BF)
            rows = pl.ds(pl.multiple_of(p * 128 + odd * 64, 64), 64)
            fr[rows, 0:256] = main
            fr[rows, 256:384] = rim
            main = main.astype(F32)
            rim = rim.astype(F32)
            mean = (
                jnp.sum(main[:, 0:128] + main[:, 128:256] + rim, axis=1, keepdims=True)
            ) * (1.0 / C)
            dm = main - mean
            dr = jnp.where(keep, rim - mean, 0.0)
            square = dm * dm
            var = jnp.sum(
                square[:, 0:128] + square[:, 128:256] + dr * dr, axis=1, keepdims=True
            ) * (1.0 / C)
            scale = lax.rsqrt(var + 1e-05)
            nm[rows, 0:256] = (
                dm * scale * gain_ref[0:1, 0:256] + bias_ref[0:1, 0:256]
            ).astype(BF)
            nm[rows, 256:384] = (
                dr * scale * gain_ref[0:1, 256:384] + bias_ref[0:1, 256:384]
            ).astype(BF)

    def norms(step, carry):
        for u in range(NORM_UNROLL):
            norm(step * NORM_UNROLL + u)
        return carry

    lax.fori_loop(0, GROUP // NORM_UNROLL, norms, 0)
    for half in range(2):
        rows = slice(half * 512, (half + 1) * 512)
        qkv[rows, :] = jnp.dot(nm[rows, :], wqkv_ref[...], preferred_element_type=F32).astype(BF)

    wide = lax.broadcasted_iota(jnp.int32, (128, 128), 1) < 64

    nt = (((1,), (1,)), ((), ()))

    ones = jnp.ones((128, 128), BF)

    def score(p):
        rows = pl.ds(pl.multiple_of(p * 128, 128), 128)
        for pair in range(2):
            q = qkv[rows, pair * 128 : (pair + 1) * 128]
            k = qkv[rows, 256 + pair * 128 : 384 + pair * 128]
            zero = jnp.zeros_like(q)
            both = jnp.concatenate([jnp.where(wide, q, zero), jnp.where(wide, zero, q)], axis=0)
            to = pl.ds(pl.multiple_of(p * 640 + pair * 256, 128), 256)
            sc[to, :] = lax.dot_general(both, k, nt, preferred_element_type=F32)
        to = pl.ds(pl.multiple_of(p * 640 + 512, 128), 128)
        sc[to, :] = lax.dot_general(
            qkv[rows, 768:896], qkv[rows, 896:1024], nt, preferred_element_type=F32
        )

    def raise_one(p):
        for at5 in range(5):
            rows = pl.ds(pl.multiple_of(p * 640 + at5 * 128, 128), 128)
            scores = sc[rows, :]
            top = jnp.max(scores, axis=1, keepdims=True)
            ex[rows, :] = jnp.exp2((scores - top) * EXP_SCALE).astype(BF)

    def gather(p):
        rows = pl.ds(pl.multiple_of(p * 128, 128), 128)
        for pair in range(2):
            v = qkv[rows, 512 + pair * 128 : 640 + pair * 128]
            to = pl.ds(pl.multiple_of(p * 640 + pair * 256, 128), 256)
            out = jnp.dot(
                ex[to, :], jnp.concatenate([v, ones], axis=1), preferred_element_type=F32
            )
            top = jnp.where(wide, out[0:128, 0:128], out[128:256, 0:128])
            under = jnp.where(wide, out[0:128, 128:256], out[128:256, 128:256])
            at[rows, pair * 128 : (pair + 1) * 128] = (top / under).astype(BF)
        to = pl.ds(pl.multiple_of(p * 640 + 512, 128), 128)
        qv = qkv[rows, 768:896]
        out = jnp.dot(ex[to, :], jnp.concatenate([qv, ones], axis=1), preferred_element_type=F32)
        at[rows, 256:384] = (out[:, 0:128] / out[:, 128:256]).astype(BF)

    def step(n, carry):
        for u in range(2):
            p = n * 2 + u
            gather(p - 2)
            raise_one(p - 1)
            score(p)
        return carry

    score(0)
    raise_one(0)
    score(1)
    lax.fori_loop(1, GROUP // 2, step, 0)
    gather(GROUP - 2)
    raise_one(GROUP - 1)
    gather(GROUP - 1)
    for half in range(2):
        rows = slice(half * 512, (half + 1) * 512)
        y = (
            fr[rows, :].astype(F32)
            + jnp.dot(at[rows, :], wout_ref[...], preferred_element_type=F32)
            + bout_ref[0:1, :]
        )
        for j in range(4):
            p = half * 4 + j
            even = y[j * 128 : j * 128 + 64]
            odd = y[j * 128 + 64 : j * 128 + 128]
            place = pl.ds(p, 64, stride=8)
            for c in range(2):
                ys[c, place, :] = even[:, c * 128 : (c + 1) * 128]
                ys[2 + c, place, :] = odd[:, c * 128 : (c + 1) * 128]
            ys[4, place, :] = jnp.where(keep, even[:, 256:384], pltpu.roll(odd[:, 256:384], 64, 1))
    for c in range(5):
        lanes = slice(c * 128, (c + 1) * 128)
        for j in range(0, 64, 2):
            two = [ys[c, n * 8 : n * 8 + 8, :] for n in ORDER[j : j + 2]]
            out_ref[j : j + 2, 0, :, lanes] = jnp.stack(two).astype(BF)


def attend_chunk(x, weights):
    count = x.shape[1]
    block = pl.BlockSpec((64, 1, 8, LANES), lambda i: (0, i, 0, 0))
    far = pl.BlockSpec(memory_space=pltpu.HBM)
    return pl.pallas_call(
        attend_kernel,
        out_shape=jax.ShapeDtypeStruct(x.shape, BF),
        grid=(count,),
        in_specs=[block, far, far, full(weights[2].shape), far, far],
        out_specs=block,
        scratch_shapes=[
            pltpu.VMEM((5, 512, 128), F32),
            pltpu.VMEM((512, 1024), BF),
            pltpu.VMEM((512, 1024), BF),
            pltpu.VMEM((512, CP), F32),
            pltpu.VMEM((512, CP), F32),
            pltpu.VMEM((1024, CP), BF),
            pltpu.VMEM((1024, CP), BF),
            pltpu.VMEM((1024, 1024), BF),
            pltpu.VMEM((1024, CP), BF),
            pltpu.VMEM((5, 512, 128), F32),
            pltpu.VMEM((5120, 128), F32),
            pltpu.VMEM((5120, 128), BF),
            pltpu.VMEM((1024, CP), BF),
            pltpu.VMEM((1024, CP), BF),
            pltpu.VMEM((CP, 1024), BF),
            pltpu.VMEM((CP, CP), BF),
            pltpu.SemaphoreType.DMA((4,)),
        ],
        compiler_params=pltpu.CompilerParams(vmem_limit_bytes=32 << 20),
        cost_estimate=pl.CostEstimate(
            flops=4000000000 * count, transcendentals=700000 * count, bytes_accessed=4000000 * count
        ),
        name="attend",
    )(x, *weights)


def final_kernel(x_ref, *rest):
    out = rest[-1]
    for i in range(CHUNK):
        y = x_ref[i * 16 : (i + 1) * 16, 0].reshape(128, LANES).T
        out[0, i, 0:256, :] = y[0:256]
        out[1, i, 0:256, :] = y[256:512]
        out[0, i, 256:320, :] = y[512:576]
        out[1, i, 256:320, :] = y[576:640]


def final_chunk(x, held, first, step, rows):
    count = x.shape[1]
    operands = [x]
    specs = [pl.BlockSpec((64, 1, 8, LANES), lambda i: (0, i, 0, 0))]
    aliases = {}
    if held is not None:
        operands.append(held)
        specs.append(pl.BlockSpec(memory_space=pl.ANY))
        aliases = {1: 0}
    return pl.pallas_call(
        final_kernel,
        out_shape=jax.ShapeDtypeStruct((2, rows, C, 128), BF),
        grid=(count,),
        in_specs=specs,
        out_specs=pl.BlockSpec((2, CHUNK, C, 128), lambda i: (0, first + i * step, 0, 0)),
        input_output_aliases=aliases,
        compiler_params=pltpu.CompilerParams(vmem_limit_bytes=16 << 20),
        cost_estimate=pl.CostEstimate(
            flops=0, transcendentals=0, bytes_accessed=1400000 * count
        ),
        name="final",
    )(*operands)


def prepare_kernel(wt_ref, wq_ref, wk_ref, wv_ref, wo_ref, *outs):
    even, odd, qkv, mix = outs
    zero = jnp.zeros((64, CP), BF)
    side = jnp.zeros((C, 64), BF)
    wide = [jnp.concatenate([wt_ref[k], side], axis=1) for k in range(3)]
    a, b, c = 256, 320, 384
    for at, tap, low, high in (
        (0, 0, 0, a),
        (c - 64, 0, a, b),
        (c, 1, 0, a),
        (640, 2, 0, a),
        (896, 1, a, b),
        (960, 2, a, b),
    ):
        even[at : at + high - low, :] = wide[tap][low:high]
    even[a:b, :] = zero
    for at, tap, low, high in (
        (0, 0, 0, a),
        (a, 1, 0, a),
        (512, 0, a, b),
        (576, 1, a, b),
        (640, 2, 0, a),
        (896, 2, a, b),
    ):
        odd[at : at + high - low, :] = wide[tap][low:high]
    odd[960:1024, :] = zero
    qkv[C:CP, :] = jnp.zeros((64, 1024), BF)
    qkv[0:C, 0:256] = wq_ref[:, 0:256]
    qkv[0:C, 256:512] = wk_ref[:, 0:256]
    qkv[0:C, 512:768] = wv_ref[:, 0:256]
    qkv[0:C, 768:896] = jnp.concatenate([wq_ref[:, 256:C], wv_ref[:, 256:C]], axis=1)
    qkv[0:C, 896:1024] = jnp.concatenate([wk_ref[:, 256:C], side], axis=1)
    out = jnp.concatenate([wo_ref[...], side], axis=1)
    mix[0:256, :] = out[0:256]
    mix[256:320, :] = zero
    mix[320:384, :] = out[256:320]


def prepared(w_temporal, w_query, w_key, w_value, w_out):
    square = full((C, C))
    shapes = ((1024, CP), (1024, CP), (CP, 1024), (CP, CP))
    return pl.pallas_call(
        prepare_kernel,
        out_shape=[pltpu.HBM(shape, BF) for shape in shapes],
        grid=(1,),
        in_specs=[full((3, C, C)), square, square, square, square],
        out_specs=[full(shape) for shape in shapes],
        compiler_params=pltpu.CompilerParams(vmem_limit_bytes=16 << 20),
        cost_estimate=pl.CostEstimate(flops=0, transcendentals=0, bytes_accessed=5000000),
        name="prepare",
    )(w_temporal, w_query, w_key, w_value, w_out)


def on_device(
    clip,
    w_spatial,
    b_spatial,
    w_temporal,
    b_temporal,
    ln_gain,
    ln_bias,
    w_query,
    w_key,
    w_value,
    w_out,
    b_out,
):
    rows = clip.shape[1]
    x = jnp.transpose(clip, (0, 1, 3, 2))
    row_count = lax.axis_size("row")
    forward = [(i, i + 1) for i in range(row_count - 1)]
    backward = [(b, a) for a, b in forward]
    low = lax.ppermute(x[:, rows - 1 :], "row", forward)
    high = lax.ppermute(x[:, :1], "row", backward)
    x = pltpu.with_memory_space_constraint(x, pltpu.HBM)
    w_spatial = pltpu.with_memory_space_constraint(w_spatial, pltpu.HBM)
    bias = b_spatial.reshape(1, C)
    w_even, w_odd, w_qkv, w_mix = prepared(w_temporal, w_query, w_key, w_value, w_out)
    vectors = jnp.pad(jnp.stack([b_temporal, ln_gain, ln_bias, b_out]), ((0, 4), (0, CP - C)))
    w_even, w_odd, w_qkv, w_mix = (
        pltpu.with_memory_space_constraint(w, pltpu.HBM) for w in (w_even, w_odd, w_qkv, w_mix)
    )
    weights = (w_even, w_odd, vectors, w_qkv, w_mix)

    def exchange(value):
        return lax.all_to_all(
            value,
            "frame",
            split_axis=0,
            concat_axis=0,
            tiled=True,
            axis_index_groups=[list(ORDER)],
        )

    held = None
    for parts in ((1,), (0, 2)):
        sent = spatial_chunk(parts, low, x, high, w_spatial, bias)
        sent = exchange(sent)
        sent = attend_chunk(sent, weights)
        sent = exchange(sent)
        held = final_chunk(sent, held, parts[0], parts[-1] - parts[0], rows)
    return jnp.transpose(held, (0, 1, 3, 2))


def solution(mesh):
    placed = (P("frame", "row", None, None),) + (P(),) * 11
    return jax.shard_map(
        on_device,
        mesh=mesh,
        in_specs=placed,
        out_specs=P("frame", "row", None, None),
        check_vma=False,
    )
```

```python
import functools

import jax
import jax.numpy as jnp
from jax import lax
from jax.experimental import pallas as pl
from jax.experimental.pallas import tpu as pltpu
from jax.sharding import PartitionSpec as P


BF = jnp.bfloat16
F32 = jnp.float32
C = 320
CP = 384
LANES = 640
CHUNK = 4
GROUP = 8
NORM_UNROLL = 2
ORDER = (
    22, 12, 52, 3, 19, 5, 60, 58, 2, 33, 10, 8, 29, 26, 25, 9,
    44, 18, 62, 11, 47, 40, 15, 39, 56, 57, 32, 23, 49, 43, 21, 45,
    42, 34, 35, 46, 20, 61, 37, 14, 63, 53, 0, 38, 27, 50, 1, 55,
    6, 13, 24, 41, 30, 28, 59, 31, 7, 16, 4, 48, 51, 54, 36, 17,
)
EXP_SCALE = 0.125 * 1.4426950408889634


def shift_rows(value, step):
    count = value.shape[0]
    turned = pltpu.roll(value, step % count, 0)
    row = lax.broadcasted_iota(jnp.int32, value.shape, 0)
    edge = 0 if step == 1 else count - 1
    return jnp.where(row == edge, 0.0, turned)


def conv_kernel(parts, rows, w_hbm, b_hbm, x_hbm, low_hbm, high_hbm, out_hbm, *scratch):
    count = len(parts)
    strips, turned, w_ref, w_even, w_odd, b_ref, out, x_sem, w_sem, o_sem = scratch
    stores = []
    loads = []
    for h, chunk in enumerate(parts):
        first, last = chunk * CHUNK - 1, (chunk + 1) * CHUNK
        for f in range(2):
            pieces = [(x_hbm.at[f, max(first, 0) : min(last, rows - 1) + 1], int(first < 0))]
            if first < 0:
                pieces.append((low_hbm.at[f], 0))
            if last == rows:
                pieces.append((high_hbm.at[f], CHUNK + 1))
            for source, at in pieces:
                loads.append(
                    pltpu.make_async_copy(
                        source,
                        strips.at[h, f, at : at + source.shape[0]],
                        x_sem.at[len(loads)],
                    )
                )
    w_loads = [pltpu.make_async_copy(w_hbm.at[a], w_ref.at[a], w_sem.at[a]) for a in range(3)]
    w_loads.append(pltpu.make_async_copy(b_hbm, b_ref, w_sem.at[3]))
    for load in loads + w_loads:
        load.start()
    for load in loads:
        load.wait()
    for h in range(count):
        for f in range(2):
            turned[h, f] = strips[h, f].reshape((CHUNK + 2) * C, 128).T
    w_even[960:1024, :] = jnp.zeros((64, 1024), BF)
    w_odd[0:64, :] = jnp.zeros((64, 1024), BF)
    for a in range(3):
        w_loads[a].wait()
        at = a * C
        for b in range(3):
            main = w_ref[a, b, :, 0:256]
            w_even[at : at + C, b * 256 : (b + 1) * 256] = main
            w_odd[64 + at : 64 + at + C, b * 256 : (b + 1) * 256] = main
        rest_w = jnp.concatenate(
            [w_ref[a, b, :, 256:C] for b in range(3)] + [jnp.zeros((C, 64), BF)], axis=1
        )
        w_even[at : at + C, 768:1024] = rest_w
        w_odd[64 + at : 64 + at + C, 768:1024] = rest_w
    lane = lax.broadcasted_iota(jnp.int32, (128, 128), 1)
    w_loads[3].wait()
    bias = b_ref[...].reshape(1, C)
    main_bias = bias[:, 0:256]
    rim_bias = jnp.concatenate([bias[:, 256:C], jnp.zeros((1, 64), F32)], axis=1)
    for h in range(count):
        for odd, weights in ((0, w_even), (1, w_odd)):
            starts = (0, 640) if odd == 0 else (256, 896)
            left = jnp.concatenate(
                [turned[h, f, :, s : s + 1024] for s in starts for f in range(2)], axis=0
            )
            y = jnp.dot(left, weights[...], preferred_element_type=F32)
            for n in range(2):
                to = slice((odd + 2 * n) * 16, (odd + 2 * n + 1) * 16)
                tails = []
                for f in range(2):
                    at = (n * 2 + f) * 128
                    part = y[at : at + 128]
                    main = (
                        shift_rows(part[:, 0:256], 1)
                        + part[:, 256:512]
                        + shift_rows(part[:, 512:768], -1)
                        + main_bias
                    )
                    out[to, h, :, f * 256 : (f + 1) * 256] = main.reshape(16, 8, 256).astype(BF)
                    pair = part[:, 768:896]
                    tails.append(
                        shift_rows(pair, 1)
                        + pltpu.roll(pair, 64, 1)
                        + shift_rows(part[:, 896:1024], -1)
                        + rim_bias
                    )
                tail = jnp.where(lane < 64, tails[0], pltpu.roll(tails[1], 64, 1))
                out[to, h, :, 512:640] = tail.reshape(16, 8, 128).astype(BF)
                store = pltpu.make_async_copy(
                    out.at[to, h], out_hbm.at[to, h], o_sem.at[len(stores)]
                )
                store.start()
                stores.append(store)
    for store in stores:
        store.wait()


def spatial_chunk(parts, low, x, high, w, b):
    count = len(parts)
    rows = x.shape[1]
    shape = (64, count, 8, LANES)
    far = pl.BlockSpec(memory_space=pltpu.HBM)
    if parts[0] > 0:
        low = x
    if (parts[-1] + 1) * CHUNK < rows:
        high = x
    return pl.pallas_call(
        functools.partial(conv_kernel, parts, rows),
        out_shape=pltpu.HBM(shape, BF),
        grid=(1,),
        in_specs=[far, far, far, far, far],
        out_specs=far,
        scratch_shapes=[
            pltpu.VMEM((count, 2, CHUNK + 2, C, 128), BF),
            pltpu.VMEM((count, 2, 128, (CHUNK + 2) * C), BF),
            pltpu.VMEM((3, 3, C, C), BF),
            pltpu.VMEM((1024, 1024), BF),
            pltpu.VMEM((1024, 1024), BF),
            pltpu.VMEM((C,), F32),
            pltpu.VMEM(shape, BF),
            pltpu.SemaphoreType.DMA((4 * count,)),
            pltpu.SemaphoreType.DMA((4,)),
            pltpu.SemaphoreType.DMA((4 * count,)),
        ],
        compiler_params=pltpu.CompilerParams(vmem_limit_bytes=32 << 20),
        cost_estimate=pl.CostEstimate(
            flops=2200000000 * count, transcendentals=0, bytes_accessed=4000000 * count
        ),
        name="spatial",
    )(w, b, x, low, high)


def full(block):
    return pl.BlockSpec(block, lambda i: (0,) * len(block))


def attend_kernel(
    x_ref, we_hbm, wo_hbm, vector_ref, wqkv_hbm, wout_hbm, out_ref, *rest
):
    *rest, we_ref, wo_ref, wqkv_ref, wout_ref, sems = rest
    loads = [
        pltpu.make_async_copy(source, target, sems.at[n])
        for n, (source, target) in enumerate(
            ((we_hbm, we_ref), (wo_hbm, wo_ref), (wqkv_hbm, wqkv_ref), (wout_hbm, wout_ref))
        )
    ]

    @pl.when(pl.program_id(0) == 0)
    def _():
        for load in loads:
            load.start()

    bt_ref, gain_ref, bias_ref, bout_ref = (vector_ref.at[i : i + 1] for i in range(4))
    xs, le, lo, fe, fo, fr, nm, qkv, at, ys, sc, ex = rest
    for c in range(5):
        lanes = slice(c * 128, (c + 1) * 128)
        for j in range(0, 64, 2):
            piece = x_ref[j : j + 2, 0, :, lanes].astype(F32)
            for n in range(2):
                to = ORDER[j + n] * 8
                xs[c, to : to + 8, :] = piece[n]
    for p in range(GROUP):
        at_rows = slice(p * 64, (p + 1) * 64)
        for c in range(5):
            here = xs[c, pl.ds(p, 64, stride=8), :]
            if c >= 2:
                before = shift_rows(here, 1).astype(BF)
                le[at_rows, (c - 2) * 128 : (c - 1) * 128] = before
            if c < 2 or c == 4:
                n = min(c, 2)
                after = shift_rows(here, -1).astype(BF)
                lo[at_rows, 640 + n * 128 : 768 + n * 128] = after
            here = here.astype(BF)
            le[at_rows, 384 + c * 128 : 512 + c * 128] = here
            lo[at_rows, c * 128 : (c + 1) * 128] = here

    @pl.when(pl.program_id(0) == 0)
    def _():
        for load in loads:
            load.wait()

    fe[...] = jnp.dot(le[...], we_ref[...], preferred_element_type=F32)
    fo[...] = jnp.dot(lo[...], wo_ref[...], preferred_element_type=F32)
    lane = lax.broadcasted_iota(jnp.int32, (64, 128), 1)
    keep = lane < 64

    def norm(p):
        rows64 = pl.ds(pl.multiple_of(p * 64, 64), 64)
        tail = le[rows64, 896:1024].astype(F32)
        for odd, total in ((0, fe), (1, fo)):
            main = (
                total[rows64, 0:256]
                + le[rows64, 384 + 256 * odd : 640 + 256 * odd].astype(F32)
                + bt_ref[0:1, 0:256]
            )
            mine = pltpu.roll(tail, 64, 1) if odd else tail
            rim = total[rows64, 256:384] + jnp.where(keep, mine, 0.0) + bt_ref[0:1, 256:384]
            main = main.astype(BF)
            rim = rim.astype(BF)
            rows = pl.ds(pl.multiple_of(p * 128 + odd * 64, 64), 64)
            fr[rows, 0:256] = main
            fr[rows, 256:384] = rim
            main = main.astype(F32)
            rim = rim.astype(F32)
            mean = (
                jnp.sum(main[:, 0:128] + main[:, 128:256] + rim, axis=1, keepdims=True)
            ) * (1.0 / C)
            dm = main - mean
            dr = jnp.where(keep, rim - mean, 0.0)
            square = dm * dm
            var = jnp.sum(
                square[:, 0:128] + square[:, 128:256] + dr * dr, axis=1, keepdims=True
            ) * (1.0 / C)
            scale = lax.rsqrt(var + 1e-05)
            nm[rows, 0:256] = (
                dm * scale * gain_ref[0:1, 0:256] + bias_ref[0:1, 0:256]
            ).astype(BF)
            nm[rows, 256:384] = (
                dr * scale * gain_ref[0:1, 256:384] + bias_ref[0:1, 256:384]
            ).astype(BF)

    def norms(step, carry):
        for u in range(NORM_UNROLL):
            norm(step * NORM_UNROLL + u)
        return carry

    lax.fori_loop(0, GROUP // NORM_UNROLL, norms, 0)
    for half in range(2):
        rows = slice(half * 512, (half + 1) * 512)
        qkv[rows, :] = jnp.dot(nm[rows, :], wqkv_ref[...], preferred_element_type=F32).astype(BF)

    wide = lax.broadcasted_iota(jnp.int32, (128, 128), 1) < 64

    nt = (((1,), (1,)), ((), ()))

    ones = jnp.ones((128, 128), BF)

    def score(p):
        rows = pl.ds(pl.multiple_of(p * 128, 128), 128)
        for pair in range(2):
            q = qkv[rows, pair * 128 : (pair + 1) * 128]
            k = qkv[rows, 256 + pair * 128 : 384 + pair * 128]
            zero = jnp.zeros_like(q)
            both = jnp.concatenate([jnp.where(wide, q, zero), jnp.where(wide, zero, q)], axis=0)
            to = pl.ds(pl.multiple_of(p * 640 + pair * 256, 128), 256)
            sc[to, :] = lax.dot_general(both, k, nt, preferred_element_type=F32)
        to = pl.ds(pl.multiple_of(p * 640 + 512, 128), 128)
        sc[to, :] = lax.dot_general(
            qkv[rows, 768:896], qkv[rows, 896:1024], nt, preferred_element_type=F32
        )

    def raise_one(p):
        for at5 in range(5):
            rows = pl.ds(pl.multiple_of(p * 640 + at5 * 128, 128), 128)
            scores = sc[rows, :]
            top = jnp.max(scores, axis=1, keepdims=True)
            ex[rows, :] = jnp.exp2((scores - top) * EXP_SCALE).astype(BF)

    def gather(p):
        rows = pl.ds(pl.multiple_of(p * 128, 128), 128)
        for pair in range(2):
            v = qkv[rows, 512 + pair * 128 : 640 + pair * 128]
            to = pl.ds(pl.multiple_of(p * 640 + pair * 256, 128), 256)
            out = jnp.dot(
                ex[to, :], jnp.concatenate([v, ones], axis=1), preferred_element_type=F32
            )
            top = jnp.where(wide, out[0:128, 0:128], out[128:256, 0:128])
            under = jnp.where(wide, out[0:128, 128:256], out[128:256, 128:256])
            at[rows, pair * 128 : (pair + 1) * 128] = (top / under).astype(BF)
        to = pl.ds(pl.multiple_of(p * 640 + 512, 128), 128)
        qv = qkv[rows, 768:896]
        out = jnp.dot(ex[to, :], jnp.concatenate([qv, ones], axis=1), preferred_element_type=F32)
        at[rows, 256:384] = (out[:, 0:128] / out[:, 128:256]).astype(BF)

    def step(n, carry):
        for u in range(2):
            p = n * 2 + u
            gather(p - 2)
            raise_one(p - 1)
            score(p)
        return carry

    score(0)
    raise_one(0)
    score(1)
    lax.fori_loop(1, GROUP // 2, step, 0)
    gather(GROUP - 2)
    raise_one(GROUP - 1)
    gather(GROUP - 1)
    for half in range(2):
        rows = slice(half * 512, (half + 1) * 512)
        y = (
            fr[rows, :].astype(F32)
            + jnp.dot(at[rows, :], wout_ref[...], preferred_element_type=F32)
            + bout_ref[0:1, :]
        )
        for j in range(4):
            p = half * 4 + j
            even = y[j * 128 : j * 128 + 64]
            odd = y[j * 128 + 64 : j * 128 + 128]
            place = pl.ds(p, 64, stride=8)
            for c in range(2):
                ys[c, place, :] = even[:, c * 128 : (c + 1) * 128]
                ys[2 + c, place, :] = odd[:, c * 128 : (c + 1) * 128]
            ys[4, place, :] = jnp.where(keep, even[:, 256:384], pltpu.roll(odd[:, 256:384], 64, 1))
    for c in range(5):
        lanes = slice(c * 128, (c + 1) * 128)
        for j in range(0, 64, 2):
            two = [ys[c, n * 8 : n * 8 + 8, :] for n in ORDER[j : j + 2]]
            out_ref[j : j + 2, 0, :, lanes] = jnp.stack(two).astype(BF)


def attend_chunk(x, weights):
    count = x.shape[1]
    block = pl.BlockSpec((64, 1, 8, LANES), lambda i: (0, i, 0, 0))
    far = pl.BlockSpec(memory_space=pltpu.HBM)
    return pl.pallas_call(
        attend_kernel,
        out_shape=jax.ShapeDtypeStruct(x.shape, BF),
        grid=(count,),
        in_specs=[block, far, far, full(weights[2].shape), far, far],
        out_specs=block,
        scratch_shapes=[
            pltpu.VMEM((5, 512, 128), F32),
            pltpu.VMEM((512, 1024), BF),
            pltpu.VMEM((512, 1024), BF),
            pltpu.VMEM((512, CP), F32),
            pltpu.VMEM((512, CP), F32),
            pltpu.VMEM((1024, CP), BF),
            pltpu.VMEM((1024, CP), BF),
            pltpu.VMEM((1024, 1024), BF),
            pltpu.VMEM((1024, CP), BF),
            pltpu.VMEM((5, 512, 128), F32),
            pltpu.VMEM((5120, 128), F32),
            pltpu.VMEM((5120, 128), BF),
            pltpu.VMEM((1024, CP), BF),
            pltpu.VMEM((1024, CP), BF),
            pltpu.VMEM((CP, 1024), BF),
            pltpu.VMEM((CP, CP), BF),
            pltpu.SemaphoreType.DMA((4,)),
        ],
        compiler_params=pltpu.CompilerParams(vmem_limit_bytes=32 << 20),
        cost_estimate=pl.CostEstimate(
            flops=4000000000 * count, transcendentals=700000 * count, bytes_accessed=4000000 * count
        ),
        name="attend",
    )(x, *weights)


def final_kernel(x_ref, *rest):
    out = rest[-1]
    for i in range(2):
        y = x_ref[i * 16 : (i + 1) * 16, 0].reshape(128, LANES).T
        out[0, i, 0:256, :] = y[0:256]
        out[1, i, 0:256, :] = y[256:512]
        out[0, i, 256:320, :] = y[512:576]
        out[1, i, 256:320, :] = y[576:640]


def final_chunk(x, held, first, step, rows):
    count = x.shape[1]
    operands = [x]
    specs = [pl.BlockSpec((32, 1, 8, LANES), lambda i: (i % 2, i // 2, 0, 0))]
    aliases = {}
    if held is not None:
        operands.append(held)
        specs.append(pl.BlockSpec(memory_space=pl.ANY))
        aliases = {1: 0}
    return pl.pallas_call(
        final_kernel,
        out_shape=jax.ShapeDtypeStruct((2, rows, C, 128), BF),
        grid=(2 * count,),
        in_specs=specs,
        out_specs=pl.BlockSpec(
            (2, 2, C, 128), lambda i: (0, 2 * (first + i // 2 * step) + i % 2, 0, 0)
        ),
        input_output_aliases=aliases,
        compiler_params=pltpu.CompilerParams(vmem_limit_bytes=16 << 20),
        cost_estimate=pl.CostEstimate(
            flops=0, transcendentals=0, bytes_accessed=1400000 * count
        ),
        name="final",
    )(*operands)


def prepare_kernel(wt_ref, wq_ref, wk_ref, wv_ref, wo_ref, *outs):
    even, odd, qkv, mix = outs
    zero = jnp.zeros((64, CP), BF)
    side = jnp.zeros((C, 64), BF)
    wide = [jnp.concatenate([wt_ref[k], side], axis=1) for k in range(3)]
    a, b, c = 256, 320, 384
    for at, tap, low, high in (
        (0, 0, 0, a),
        (c - 64, 0, a, b),
        (c, 1, 0, a),
        (640, 2, 0, a),
        (896, 1, a, b),
        (960, 2, a, b),
    ):
        even[at : at + high - low, :] = wide[tap][low:high]
    even[a:b, :] = zero
    for at, tap, low, high in (
        (0, 0, 0, a),
        (a, 1, 0, a),
        (512, 0, a, b),
        (576, 1, a, b),
        (640, 2, 0, a),
        (896, 2, a, b),
    ):
        odd[at : at + high - low, :] = wide[tap][low:high]
    odd[960:1024, :] = zero
    qkv[C:CP, :] = jnp.zeros((64, 1024), BF)
    qkv[0:C, 0:256] = wq_ref[:, 0:256]
    qkv[0:C, 256:512] = wk_ref[:, 0:256]
    qkv[0:C, 512:768] = wv_ref[:, 0:256]
    qkv[0:C, 768:896] = jnp.concatenate([wq_ref[:, 256:C], wv_ref[:, 256:C]], axis=1)
    qkv[0:C, 896:1024] = jnp.concatenate([wk_ref[:, 256:C], side], axis=1)
    out = jnp.concatenate([wo_ref[...], side], axis=1)
    mix[0:256, :] = out[0:256]
    mix[256:320, :] = zero
    mix[320:384, :] = out[256:320]


def prepared(w_temporal, w_query, w_key, w_value, w_out):
    square = full((C, C))
    shapes = ((1024, CP), (1024, CP), (CP, 1024), (CP, CP))
    return pl.pallas_call(
        prepare_kernel,
        out_shape=[pltpu.HBM(shape, BF) for shape in shapes],
        grid=(1,),
        in_specs=[full((3, C, C)), square, square, square, square],
        out_specs=[full(shape) for shape in shapes],
        compiler_params=pltpu.CompilerParams(vmem_limit_bytes=16 << 20),
        cost_estimate=pl.CostEstimate(flops=0, transcendentals=0, bytes_accessed=5000000),
        name="prepare",
    )(w_temporal, w_query, w_key, w_value, w_out)


def on_device(
    clip,
    w_spatial,
    b_spatial,
    w_temporal,
    b_temporal,
    ln_gain,
    ln_bias,
    w_query,
    w_key,
    w_value,
    w_out,
    b_out,
):
    rows = clip.shape[1]
    x = jnp.transpose(clip, (0, 1, 3, 2))
    row_count = lax.axis_size("row")
    forward = [(i, i + 1) for i in range(row_count - 1)]
    backward = [(b, a) for a, b in forward]
    low = lax.ppermute(x[:, rows - 1 :], "row", forward)
    high = lax.ppermute(x[:, :1], "row", backward)
    x = pltpu.with_memory_space_constraint(x, pltpu.HBM)
    w_spatial = pltpu.with_memory_space_constraint(w_spatial, pltpu.HBM)
    bias = pltpu.with_memory_space_constraint(b_spatial, pltpu.HBM)
    w_even, w_odd, w_qkv, w_mix = prepared(w_temporal, w_query, w_key, w_value, w_out)
    vectors = jnp.pad(jnp.stack([b_temporal, ln_gain, ln_bias, b_out]), ((0, 4), (0, CP - C)))
    w_even, w_odd, w_qkv, w_mix = (
        pltpu.with_memory_space_constraint(w, pltpu.HBM) for w in (w_even, w_odd, w_qkv, w_mix)
    )
    weights = (w_even, w_odd, vectors, w_qkv, w_mix)

    def exchange(value):
        return lax.all_to_all(
            value,
            "frame",
            split_axis=0,
            concat_axis=0,
            tiled=True,
            axis_index_groups=[list(ORDER)],
        )

    held = None
    for parts in ((1,), (0, 2)):
        sent = spatial_chunk(parts, low, x, high, w_spatial, bias)
        sent = exchange(sent)
        sent = attend_chunk(sent, weights)
        sent = exchange(sent)
        held = final_chunk(sent, held, parts[0], parts[-1] - parts[0], rows)
    return jnp.transpose(held, (0, 1, 3, 2))


def solution(mesh):
    placed = (P("frame", "row", None, None),) + (P(),) * 11
    return jax.shard_map(
        on_device,
        mesh=mesh,
        in_specs=placed,
        out_specs=P("frame", "row", None, None),
        check_vma=False,
    )
```

```python
import functools

import jax
import jax.numpy as jnp
from jax import lax
from jax.experimental import pallas as pl
from jax.experimental.pallas import tpu as pltpu
from jax.sharding import PartitionSpec as P


BF = jnp.bfloat16
F32 = jnp.float32
C = 320
CP = 384
LANES = 640
CHUNK = 4
GROUP = 8
NORM_UNROLL = 2
ORDER = (
    22, 12, 52, 3, 19, 5, 60, 58, 2, 33, 10, 8, 29, 26, 25, 9,
    44, 18, 62, 11, 47, 40, 15, 39, 56, 57, 32, 23, 49, 43, 21, 45,
    42, 34, 35, 46, 20, 61, 37, 14, 63, 53, 0, 38, 27, 50, 1, 55,
    6, 13, 24, 41, 30, 28, 59, 31, 7, 16, 4, 48, 51, 54, 36, 17,
)
EXP_SCALE = 0.125 * 1.4426950408889634


def shift_rows(value, step):
    count = value.shape[0]
    turned = pltpu.roll(value, step % count, 0)
    row = lax.broadcasted_iota(jnp.int32, value.shape, 0)
    edge = 0 if step == 1 else count - 1
    return jnp.where(row == edge, 0.0, turned)


def conv_kernel(parts, rows, w_hbm, b_hbm, x_hbm, low_hbm, high_hbm, out_hbm, *scratch):
    count = len(parts)
    strips, turned, w_ref, w_even, w_odd, b_ref, out, x_sem, w_sem, o_sem = scratch
    stores = []
    loads = []
    for h, chunk in enumerate(parts):
        first, last = chunk * CHUNK - 1, (chunk + 1) * CHUNK
        for f in range(2):
            pieces = [(x_hbm.at[f, max(first, 0) : min(last, rows - 1) + 1], int(first < 0))]
            if first < 0:
                pieces.append((low_hbm.at[f], 0))
            if last == rows:
                pieces.append((high_hbm.at[f], CHUNK + 1))
            for source, at in pieces:
                loads.append(
                    pltpu.make_async_copy(
                        source,
                        strips.at[h, f, at : at + source.shape[0]],
                        x_sem.at[len(loads)],
                    )
                )
    w_loads = [pltpu.make_async_copy(w_hbm.at[a], w_ref.at[a], w_sem.at[a]) for a in range(3)]
    w_loads.append(pltpu.make_async_copy(b_hbm, b_ref, w_sem.at[3]))
    for load in loads + w_loads:
        load.start()
    for load in loads:
        load.wait()
    for h in range(count):
        for f in range(2):
            turned[h, f] = strips[h, f].reshape((CHUNK + 2) * C, 128).T
    w_even[960:1024, :] = jnp.zeros((64, 1024), BF)
    w_odd[0:64, :] = jnp.zeros((64, 1024), BF)
    for a in range(3):
        w_loads[a].wait()
        at = a * C
        for b in range(3):
            main = w_ref[a, b, :, 0:256]
            w_even[at : at + C, b * 256 : (b + 1) * 256] = main
            w_odd[64 + at : 64 + at + C, b * 256 : (b + 1) * 256] = main
        rest_w = jnp.concatenate(
            [w_ref[a, b, :, 256:C] for b in range(3)] + [jnp.zeros((C, 64), BF)], axis=1
        )
        w_even[at : at + C, 768:1024] = rest_w
        w_odd[64 + at : 64 + at + C, 768:1024] = rest_w
    lane = lax.broadcasted_iota(jnp.int32, (128, 128), 1)
    w_loads[3].wait()
    bias = b_ref[...].reshape(1, C)
    main_bias = bias[:, 0:256]
    rim_bias = jnp.concatenate([bias[:, 256:C], jnp.zeros((1, 64), F32)], axis=1)
    for h in range(count):
        for odd, weights in ((0, w_even), (1, w_odd)):
            starts = (0, 640) if odd == 0 else (256, 896)
            left = jnp.concatenate(
                [turned[h, f, :, s : s + 1024] for s in starts for f in range(2)], axis=0
            )
            y = jnp.dot(left, weights[...], preferred_element_type=F32)
            for n in range(2):
                to = slice((odd + 2 * n) * 16, (odd + 2 * n + 1) * 16)
                tails = []
                for f in range(2):
                    at = (n * 2 + f) * 128
                    part = y[at : at + 128]
                    main = (
                        shift_rows(part[:, 0:256], 1)
                        + part[:, 256:512]
                        + shift_rows(part[:, 512:768], -1)
                        + main_bias
                    )
                    out[to, h, :, f * 256 : (f + 1) * 256] = main.reshape(16, 8, 256).astype(BF)
                    pair = part[:, 768:896]
                    tails.append(
                        shift_rows(pair, 1)
                        + pltpu.roll(pair, 64, 1)
                        + shift_rows(part[:, 896:1024], -1)
                        + rim_bias
                    )
                tail = jnp.where(lane < 64, tails[0], pltpu.roll(tails[1], 64, 1))
                out[to, h, :, 512:640] = tail.reshape(16, 8, 128).astype(BF)
                store = pltpu.make_async_copy(
                    out.at[to, h], out_hbm.at[to, h], o_sem.at[len(stores)]
                )
                store.start()
                stores.append(store)
    for store in stores:
        store.wait()


def spatial_chunk(parts, low, x, high, w, b):
    count = len(parts)
    rows = x.shape[1]
    shape = (64, count, 8, LANES)
    far = pl.BlockSpec(memory_space=pltpu.HBM)
    if parts[0] > 0:
        low = x
    if (parts[-1] + 1) * CHUNK < rows:
        high = x
    return pl.pallas_call(
        functools.partial(conv_kernel, parts, rows),
        out_shape=pltpu.HBM(shape, BF),
        grid=(1,),
        in_specs=[far, far, far, far, far],
        out_specs=far,
        scratch_shapes=[
            pltpu.VMEM((count, 2, CHUNK + 2, C, 128), BF),
            pltpu.VMEM((count, 2, 128, (CHUNK + 2) * C), BF),
            pltpu.VMEM((3, 3, C, C), BF),
            pltpu.VMEM((1024, 1024), BF),
            pltpu.VMEM((1024, 1024), BF),
            pltpu.VMEM((C,), F32),
            pltpu.VMEM(shape, BF),
            pltpu.SemaphoreType.DMA((4 * count,)),
            pltpu.SemaphoreType.DMA((4,)),
            pltpu.SemaphoreType.DMA((4 * count,)),
        ],
        compiler_params=pltpu.CompilerParams(vmem_limit_bytes=32 << 20),
        cost_estimate=pl.CostEstimate(
            flops=2200000000 * count, transcendentals=0, bytes_accessed=4000000 * count
        ),
        name="spatial",
    )(w, b, x, low, high)


def full(block):
    return pl.BlockSpec(block, lambda i: (0,) * len(block))


def attend_kernel(
    x_ref, we_hbm, wo_hbm, vector_ref, wqkv_hbm, wout_hbm, out_ref, *rest
):
    *rest, we_ref, wo_ref, wqkv_ref, wout_ref, sems = rest
    loads = [
        pltpu.make_async_copy(source, target, sems.at[n])
        for n, (source, target) in enumerate(
            ((we_hbm, we_ref), (wo_hbm, wo_ref), (wqkv_hbm, wqkv_ref), (wout_hbm, wout_ref))
        )
    ]

    @pl.when(pl.program_id(0) == 0)
    def _():
        for load in loads:
            load.start()

    bt_ref, gain_ref, bias_ref, bout_ref = (vector_ref.at[i : i + 1] for i in range(4))
    xs, le, lo, fe, fo, fr, nm, qkv, at, ys, sc, ex = rest
    for c in range(5):
        lanes = slice(c * 128, (c + 1) * 128)
        for j in range(0, 64, 2):
            piece = x_ref[j : j + 2, 0, :, lanes].astype(F32)
            for n in range(2):
                to = ORDER[j + n] * 8
                xs[c, to : to + 8, :] = piece[n]
    for p in range(GROUP):
        at_rows = slice(p * 64, (p + 1) * 64)
        for c in range(5):
            here = xs[c, pl.ds(p, 64, stride=8), :]
            if c >= 2:
                before = shift_rows(here, 1).astype(BF)
                le[at_rows, (c - 2) * 128 : (c - 1) * 128] = before
            if c < 2 or c == 4:
                n = min(c, 2)
                after = shift_rows(here, -1).astype(BF)
                lo[at_rows, 640 + n * 128 : 768 + n * 128] = after
            here = here.astype(BF)
            le[at_rows, 384 + c * 128 : 512 + c * 128] = here
            lo[at_rows, c * 128 : (c + 1) * 128] = here

    @pl.when(pl.program_id(0) == 0)
    def _():
        for load in loads:
            load.wait()

    fe[...] = jnp.dot(le[...], we_ref[...], preferred_element_type=F32)
    fo[...] = jnp.dot(lo[...], wo_ref[...], preferred_element_type=F32)
    lane = lax.broadcasted_iota(jnp.int32, (64, 128), 1)
    keep = lane < 64

    def norm(p):
        rows64 = pl.ds(pl.multiple_of(p * 64, 64), 64)
        tail = le[rows64, 896:1024].astype(F32)
        for odd, total in ((0, fe), (1, fo)):
            main = (
                total[rows64, 0:256]
                + le[rows64, 384 + 256 * odd : 640 + 256 * odd].astype(F32)
                + bt_ref[0:1, 0:256]
            )
            mine = pltpu.roll(tail, 64, 1) if odd else tail
            rim = total[rows64, 256:384] + jnp.where(keep, mine, 0.0) + bt_ref[0:1, 256:384]
            main = main.astype(BF)
            rim = rim.astype(BF)
            rows = pl.ds(pl.multiple_of(p * 128 + odd * 64, 64), 64)
            fr[rows, 0:256] = main
            fr[rows, 256:384] = rim
            main = main.astype(F32)
            rim = rim.astype(F32)
            mean = (
                jnp.sum(main[:, 0:128] + main[:, 128:256] + rim, axis=1, keepdims=True)
            ) * (1.0 / C)
            dm = main - mean
            dr = jnp.where(keep, rim - mean, 0.0)
            square = dm * dm
            var = jnp.sum(
                square[:, 0:128] + square[:, 128:256] + dr * dr, axis=1, keepdims=True
            ) * (1.0 / C)
            scale = lax.rsqrt(var + 1e-05)
            nm[rows, 0:256] = (
                dm * scale * gain_ref[0:1, 0:256] + bias_ref[0:1, 0:256]
            ).astype(BF)
            nm[rows, 256:384] = (
                dr * scale * gain_ref[0:1, 256:384] + bias_ref[0:1, 256:384]
            ).astype(BF)

    def norms(step, carry):
        for u in range(NORM_UNROLL):
            norm(step * NORM_UNROLL + u)
        return carry

    lax.fori_loop(0, GROUP // NORM_UNROLL, norms, 0)
    for half in range(2):
        rows = slice(half * 512, (half + 1) * 512)
        qkv[rows, :] = jnp.dot(nm[rows, :], wqkv_ref[...], preferred_element_type=F32).astype(BF)

    wide = lax.broadcasted_iota(jnp.int32, (128, 128), 1) < 64

    nt = (((1,), (1,)), ((), ()))

    ones = jnp.ones((128, 128), BF)

    def score(p):
        rows = pl.ds(pl.multiple_of(p * 128, 128), 128)
        for pair in range(2):
            q = qkv[rows, pair * 128 : (pair + 1) * 128]
            k = qkv[rows, 256 + pair * 128 : 384 + pair * 128]
            zero = jnp.zeros_like(q)
            both = jnp.concatenate([jnp.where(wide, q, zero), jnp.where(wide, zero, q)], axis=0)
            to = pl.ds(pl.multiple_of(p * 640 + pair * 256, 128), 256)
            sc[to, :] = lax.dot_general(both, k, nt, preferred_element_type=F32)
        to = pl.ds(pl.multiple_of(p * 640 + 512, 128), 128)
        sc[to, :] = lax.dot_general(
            qkv[rows, 768:896], qkv[rows, 896:1024], nt, preferred_element_type=F32
        )

    def raise_one(p):
        for at5 in range(5):
            rows = pl.ds(pl.multiple_of(p * 640 + at5 * 128, 128), 128)
            scores = sc[rows, :]
            top = jnp.max(scores, axis=1, keepdims=True)
            ex[rows, :] = jnp.exp2((scores - top) * EXP_SCALE).astype(BF)

    def gather(p):
        rows = pl.ds(pl.multiple_of(p * 128, 128), 128)
        for pair in range(2):
            v = qkv[rows, 512 + pair * 128 : 640 + pair * 128]
            to = pl.ds(pl.multiple_of(p * 640 + pair * 256, 128), 256)
            out = jnp.dot(
                ex[to, :], jnp.concatenate([v, ones], axis=1), preferred_element_type=F32
            )
            top = jnp.where(wide, out[0:128, 0:128], out[128:256, 0:128])
            under = jnp.where(wide, out[0:128, 128:256], out[128:256, 128:256])
            at[rows, pair * 128 : (pair + 1) * 128] = (top / under).astype(BF)
        to = pl.ds(pl.multiple_of(p * 640 + 512, 128), 128)
        qv = qkv[rows, 768:896]
        out = jnp.dot(ex[to, :], jnp.concatenate([qv, ones], axis=1), preferred_element_type=F32)
        at[rows, 256:384] = (out[:, 0:128] / out[:, 128:256]).astype(BF)

    def step(n, carry):
        for u in range(2):
            p = n * 2 + u
            gather(p - 2)
            raise_one(p - 1)
            score(p)
        return carry

    score(0)
    raise_one(0)
    score(1)
    lax.fori_loop(1, GROUP // 2, step, 0)
    gather(GROUP - 2)
    raise_one(GROUP - 1)
    gather(GROUP - 1)
    for half in range(2):
        rows = slice(half * 512, (half + 1) * 512)
        y = (
            fr[rows, :].astype(F32)
            + jnp.dot(at[rows, :], wout_ref[...], preferred_element_type=F32)
            + bout_ref[0:1, :]
        )
        for j in range(4):
            p = half * 4 + j
            even = y[j * 128 : j * 128 + 64]
            odd = y[j * 128 + 64 : j * 128 + 128]
            place = pl.ds(p, 64, stride=8)
            for c in range(2):
                ys[c, place, :] = even[:, c * 128 : (c + 1) * 128]
                ys[2 + c, place, :] = odd[:, c * 128 : (c + 1) * 128]
            ys[4, place, :] = jnp.where(keep, even[:, 256:384], pltpu.roll(odd[:, 256:384], 64, 1))
    for c in range(5):
        lanes = slice(c * 128, (c + 1) * 128)
        for j in range(0, 64, 2):
            two = [ys[c, n * 8 : n * 8 + 8, :] for n in ORDER[j : j + 2]]
            out_ref[j : j + 2, 0, :, lanes] = jnp.stack(two).astype(BF)


def attend_chunk(x, weights):
    count = x.shape[1]
    block = pl.BlockSpec((64, 1, 8, LANES), lambda i: (0, i, 0, 0))
    far = pl.BlockSpec(memory_space=pltpu.HBM)
    return pl.pallas_call(
        attend_kernel,
        out_shape=jax.ShapeDtypeStruct(x.shape, BF),
        grid=(count,),
        in_specs=[block, far, far, full(weights[2].shape), far, far],
        out_specs=block,
        scratch_shapes=[
            pltpu.VMEM((5, 512, 128), F32),
            pltpu.VMEM((512, 1024), BF),
            pltpu.VMEM((512, 1024), BF),
            pltpu.VMEM((512, CP), F32),
            pltpu.VMEM((512, CP), F32),
            pltpu.VMEM((1024, CP), BF),
            pltpu.VMEM((1024, CP), BF),
            pltpu.VMEM((1024, 1024), BF),
            pltpu.VMEM((1024, CP), BF),
            pltpu.VMEM((5, 512, 128), F32),
            pltpu.VMEM((5120, 128), F32),
            pltpu.VMEM((5120, 128), BF),
            pltpu.VMEM((1024, CP), BF),
            pltpu.VMEM((1024, CP), BF),
            pltpu.VMEM((CP, 1024), BF),
            pltpu.VMEM((CP, CP), BF),
            pltpu.SemaphoreType.DMA((4,)),
        ],
        compiler_params=pltpu.CompilerParams(vmem_limit_bytes=32 << 20),
        cost_estimate=pl.CostEstimate(
            flops=4000000000 * count, transcendentals=700000 * count, bytes_accessed=4000000 * count
        ),
        name="attend",
    )(x, *weights)


def final_kernel(x_ref, *rest):
    out = rest[-1]
    for i in range(CHUNK):
        y = x_ref[i * 16 : (i + 1) * 16, 0].reshape(128, LANES).T
        out[0, i, 0:256, :] = y[0:256]
        out[1, i, 0:256, :] = y[256:512]
        out[0, i, 256:320, :] = y[512:576]
        out[1, i, 256:320, :] = y[576:640]


def final_chunk(x, held, first, step, rows):
    count = x.shape[1]
    operands = [x]
    specs = [pl.BlockSpec((64, 1, 8, LANES), lambda i: (0, i, 0, 0))]
    aliases = {}
    if held is not None:
        operands.append(held)
        specs.append(pl.BlockSpec(memory_space=pl.ANY))
        aliases = {1: 0}
    return pl.pallas_call(
        final_kernel,
        out_shape=jax.ShapeDtypeStruct((2, rows, C, 128), BF),
        grid=(count,),
        in_specs=specs,
        out_specs=pl.BlockSpec((2, CHUNK, C, 128), lambda i: (0, first + i * step, 0, 0)),
        input_output_aliases=aliases,
        compiler_params=pltpu.CompilerParams(vmem_limit_bytes=16 << 20),
        cost_estimate=pl.CostEstimate(
            flops=0, transcendentals=0, bytes_accessed=1400000 * count
        ),
        name="final",
    )(*operands)


def prepare_kernel(wt_ref, wq_ref, wk_ref, wv_ref, wo_ref, *outs):
    even, odd, qkv, mix = outs
    zero = jnp.zeros((64, CP), BF)
    side = jnp.zeros((C, 64), BF)
    wide = [jnp.concatenate([wt_ref[k], side], axis=1) for k in range(3)]
    a, b, c = 256, 320, 384
    for at, tap, low, high in (
        (0, 0, 0, a),
        (c - 64, 0, a, b),
        (c, 1, 0, a),
        (640, 2, 0, a),
        (896, 1, a, b),
        (960, 2, a, b),
    ):
        even[at : at + high - low, :] = wide[tap][low:high]
    even[a:b, :] = zero
    for at, tap, low, high in (
        (0, 0, 0, a),
        (a, 1, 0, a),
        (512, 0, a, b),
        (576, 1, a, b),
        (640, 2, 0, a),
        (896, 2, a, b),
    ):
        odd[at : at + high - low, :] = wide[tap][low:high]
    odd[960:1024, :] = zero
    qkv[C:CP, :] = jnp.zeros((64, 1024), BF)
    qkv[0:C, 0:256] = wq_ref[:, 0:256]
    qkv[0:C, 256:512] = wk_ref[:, 0:256]
    qkv[0:C, 512:768] = wv_ref[:, 0:256]
    qkv[0:C, 768:896] = jnp.concatenate([wq_ref[:, 256:C], wv_ref[:, 256:C]], axis=1)
    qkv[0:C, 896:1024] = jnp.concatenate([wk_ref[:, 256:C], side], axis=1)
    out = jnp.concatenate([wo_ref[...], side], axis=1)
    mix[0:256, :] = out[0:256]
    mix[256:320, :] = zero
    mix[320:384, :] = out[256:320]


def prepared(w_temporal, w_query, w_key, w_value, w_out):
    square = full((C, C))
    shapes = ((1024, CP), (1024, CP), (CP, 1024), (CP, CP))
    return pl.pallas_call(
        prepare_kernel,
        out_shape=[pltpu.HBM(shape, BF) for shape in shapes],
        grid=(1,),
        in_specs=[full((3, C, C)), square, square, square, square],
        out_specs=[full(shape) for shape in shapes],
        compiler_params=pltpu.CompilerParams(vmem_limit_bytes=16 << 20),
        cost_estimate=pl.CostEstimate(flops=0, transcendentals=0, bytes_accessed=5000000),
        name="prepare",
    )(w_temporal, w_query, w_key, w_value, w_out)


def on_device(
    clip,
    w_spatial,
    b_spatial,
    w_temporal,
    b_temporal,
    ln_gain,
    ln_bias,
    w_query,
    w_key,
    w_value,
    w_out,
    b_out,
):
    rows = clip.shape[1]
    x = jnp.transpose(clip, (0, 1, 3, 2))
    row_count = lax.axis_size("row")
    forward = [(i, i + 1) for i in range(row_count - 1)]
    backward = [(b, a) for a, b in forward]
    low = lax.ppermute(x[:, rows - 1 :], "row", forward)
    high = lax.ppermute(x[:, :1], "row", backward)
    x = pltpu.with_memory_space_constraint(x, pltpu.HBM)
    w_spatial = pltpu.with_memory_space_constraint(w_spatial, pltpu.HBM)
    bias = pltpu.with_memory_space_constraint(b_spatial, pltpu.HBM)
    w_even, w_odd, w_qkv, w_mix = prepared(w_temporal, w_query, w_key, w_value, w_out)
    vectors = jnp.pad(jnp.stack([b_temporal, ln_gain, ln_bias, b_out]), ((0, 4), (0, CP - C)))
    w_even, w_odd, w_qkv, w_mix = (
        pltpu.with_memory_space_constraint(w, pltpu.HBM) for w in (w_even, w_odd, w_qkv, w_mix)
    )
    weights = (w_even, w_odd, vectors, w_qkv, w_mix)

    def exchange(value):
        return lax.all_to_all(
            value,
            "frame",
            split_axis=0,
            concat_axis=0,
            tiled=True,
            axis_index_groups=[list(ORDER)],
        )

    held = None
    for parts in ((1,), (0, 2)):
        sent = spatial_chunk(parts, low, x, high, w_spatial, bias)
        sent = exchange(sent)
        sent = attend_chunk(sent, weights)
        sent = exchange(sent)
        held = final_chunk(sent, held, parts[0], parts[-1] - parts[0], rows)
    return jnp.transpose(held, (0, 1, 3, 2))


def solution(mesh):
    placed = (P("frame", "row", None, None),) + (P(),) * 11
    return jax.shard_map(
        on_device,
        mesh=mesh,
        in_specs=placed,
        out_specs=P("frame", "row", None, None),
        check_vma=False,
    )
```

```python
import functools

import jax
import jax.numpy as jnp
from jax import lax
from jax.experimental import pallas as pl
from jax.experimental.pallas import tpu as pltpu
from jax.sharding import PartitionSpec as P


BF = jnp.bfloat16
F32 = jnp.float32
C = 320
CP = 384
LANES = 640
CHUNK = 4
GROUP = 8
NORM_UNROLL = 2
ORDER = (
    22, 12, 52, 3, 19, 5, 60, 58, 2, 33, 10, 8, 29, 26, 25, 9,
    44, 18, 62, 11, 47, 40, 15, 39, 56, 57, 32, 23, 49, 43, 21, 45,
    42, 34, 35, 46, 20, 61, 37, 14, 63, 53, 0, 38, 27, 50, 1, 55,
    6, 13, 24, 41, 30, 28, 59, 31, 7, 16, 4, 48, 51, 54, 36, 17,
)
EXP_SCALE = 0.125 * 1.4426950408889634


def shift_rows(value, step):
    count = value.shape[0]
    turned = pltpu.roll(value, step % count, 0)
    row = lax.broadcasted_iota(jnp.int32, value.shape, 0)
    edge = 0 if step == 1 else count - 1
    return jnp.where(row == edge, 0.0, turned)


def conv_kernel(parts, rows, w_hbm, b_hbm, x_hbm, low_hbm, high_hbm, out_hbm, *scratch):
    count = len(parts)
    strips, turned, w_ref, w_even, w_odd, b_ref, out, x_sem, w_sem, o_sem = scratch
    stores = []
    loads = []
    for h, chunk in enumerate(parts):
        first, last = chunk * CHUNK - 1, (chunk + 1) * CHUNK
        for f in range(2):
            pieces = [(x_hbm.at[f, max(first, 0) : min(last, rows - 1) + 1], int(first < 0))]
            if first < 0:
                pieces.append((low_hbm.at[f], 0))
            if last == rows:
                pieces.append((high_hbm.at[f], CHUNK + 1))
            for source, at in pieces:
                loads.append(
                    pltpu.make_async_copy(
                        source,
                        strips.at[h, f, at : at + source.shape[0]],
                        x_sem.at[len(loads)],
                    )
                )
    w_loads = [pltpu.make_async_copy(w_hbm.at[a], w_ref.at[a], w_sem.at[a]) for a in range(3)]
    w_loads.append(pltpu.make_async_copy(b_hbm, b_ref, w_sem.at[3]))
    for load in loads + w_loads:
        load.start()
    for load in loads:
        load.wait()
    for h in range(count):
        for f in range(2):
            turned[h, f] = strips[h, f].reshape((CHUNK + 2) * C, 128).T
    w_even[960:1024, :] = jnp.zeros((64, 1024), BF)
    w_odd[0:64, :] = jnp.zeros((64, 1024), BF)
    for a in range(3):
        w_loads[a].wait()
        at = a * C
        for b in range(3):
            main = w_ref[a, b, :, 0:256]
            w_even[at : at + C, b * 256 : (b + 1) * 256] = main
            w_odd[64 + at : 64 + at + C, b * 256 : (b + 1) * 256] = main
        rest_w = jnp.concatenate(
            [w_ref[a, b, :, 256:C] for b in range(3)] + [jnp.zeros((C, 64), BF)], axis=1
        )
        w_even[at : at + C, 768:1024] = rest_w
        w_odd[64 + at : 64 + at + C, 768:1024] = rest_w
    lane = lax.broadcasted_iota(jnp.int32, (128, 128), 1)
    w_loads[3].wait()
    bias = b_ref[...].reshape(1, C)
    main_bias = bias[:, 0:256]
    rim_bias = jnp.concatenate([bias[:, 256:C], jnp.zeros((1, 64), F32)], axis=1)
    for h in range(count):
        for odd, weights in ((0, w_even), (1, w_odd)):
            starts = (0, 640) if odd == 0 else (256, 896)
            left = jnp.concatenate(
                [turned[h, f, :, s : s + 1024] for s in starts for f in range(2)], axis=0
            )
            y = jnp.dot(left, weights[...], preferred_element_type=F32)
            for n in range(2):
                to = slice((odd + 2 * n) * 16, (odd + 2 * n + 1) * 16)
                tails = []
                for f in range(2):
                    at = (n * 2 + f) * 128
                    part = y[at : at + 128]
                    main = (
                        shift_rows(part[:, 0:256], 1)
                        + part[:, 256:512]
                        + shift_rows(part[:, 512:768], -1)
                        + main_bias
                    )
                    out[to, h, :, f * 256 : (f + 1) * 256] = main.reshape(16, 8, 256).astype(BF)
                    pair = part[:, 768:896]
                    tails.append(
                        shift_rows(pair, 1)
                        + pltpu.roll(pair, 64, 1)
                        + shift_rows(part[:, 896:1024], -1)
                        + rim_bias
                    )
                tail = jnp.where(lane < 64, tails[0], pltpu.roll(tails[1], 64, 1))
                out[to, h, :, 512:640] = tail.reshape(16, 8, 128).astype(BF)
                store = pltpu.make_async_copy(
                    out.at[to, h], out_hbm.at[to, h], o_sem.at[len(stores)]
                )
                store.start()
                stores.append(store)
    for store in stores:
        store.wait()


def spatial_chunk(parts, low, x, high, w, b):
    count = len(parts)
    rows = x.shape[1]
    shape = (64, count, 8, LANES)
    far = pl.BlockSpec(memory_space=pltpu.HBM)
    if parts[0] > 0:
        low = x
    if (parts[-1] + 1) * CHUNK < rows:
        high = x
    return pl.pallas_call(
        functools.partial(conv_kernel, parts, rows),
        out_shape=pltpu.HBM(shape, BF),
        grid=(1,),
        in_specs=[far, far, far, far, far],
        out_specs=far,
        scratch_shapes=[
            pltpu.VMEM((count, 2, CHUNK + 2, C, 128), BF),
            pltpu.VMEM((count, 2, 128, (CHUNK + 2) * C), BF),
            pltpu.VMEM((3, 3, C, C), BF),
            pltpu.VMEM((1024, 1024), BF),
            pltpu.VMEM((1024, 1024), BF),
            pltpu.VMEM((C,), F32),
            pltpu.VMEM(shape, BF),
            pltpu.SemaphoreType.DMA((4 * count,)),
            pltpu.SemaphoreType.DMA((4,)),
            pltpu.SemaphoreType.DMA((4 * count,)),
        ],
        compiler_params=pltpu.CompilerParams(vmem_limit_bytes=32 << 20),
        cost_estimate=pl.CostEstimate(
            flops=2200000000 * count, transcendentals=0, bytes_accessed=4000000 * count
        ),
        name="spatial",
    )(w, b, x, low, high)


def full(block):
    return pl.BlockSpec(block, lambda i: (0,) * len(block))


def attend_kernel(
    x_ref, we_hbm, wo_hbm, vector_ref, wqkv_hbm, wout_hbm, out_ref, *rest
):
    *rest, we_ref, wo_ref, wqkv_ref, wout_ref, sems = rest
    loads = [
        pltpu.make_async_copy(source, target, sems.at[n])
        for n, (source, target) in enumerate(
            ((we_hbm, we_ref), (wo_hbm, wo_ref), (wqkv_hbm, wqkv_ref), (wout_hbm, wout_ref))
        )
    ]

    @pl.when(pl.program_id(0) == 0)
    def _():
        for load in loads:
            load.start()

    bt_ref, gain_ref, bias_ref, bout_ref = (vector_ref.at[i : i + 1] for i in range(4))
    xs, le, lo, fe, fo, fr, nm, qkv, at, ys, sc, ex = rest
    for c in range(5):
        lanes = slice(c * 128, (c + 1) * 128)
        for j in range(0, 64, 2):
            piece = x_ref[j : j + 2, 0, :, lanes].astype(F32)
            for n in range(2):
                to = ORDER[j + n] * 8
                xs[c, to : to + 8, :] = piece[n]
    for p in range(GROUP):
        at_rows = slice(p * 64, (p + 1) * 64)
        for c in range(5):
            here = xs[c, pl.ds(p, 64, stride=8), :]
            if c >= 2:
                before = shift_rows(here, 1).astype(BF)
                le[at_rows, (c - 2) * 128 : (c - 1) * 128] = before
            if c < 2 or c == 4:
                n = min(c, 2)
                after = shift_rows(here, -1).astype(BF)
                lo[at_rows, 640 + n * 128 : 768 + n * 128] = after
            here = here.astype(BF)
            le[at_rows, 384 + c * 128 : 512 + c * 128] = here
            lo[at_rows, c * 128 : (c + 1) * 128] = here

    @pl.when(pl.program_id(0) == 0)
    def _():
        for load in loads:
            load.wait()

    fe[...] = jnp.dot(le[...], we_ref[...], preferred_element_type=F32)
    fo[...] = jnp.dot(lo[...], wo_ref[...], preferred_element_type=F32)
    lane = lax.broadcasted_iota(jnp.int32, (64, 128), 1)
    keep = lane < 64

    def norm(p):
        rows64 = pl.ds(pl.multiple_of(p * 64, 64), 64)
        tail = le[rows64, 896:1024].astype(F32)
        for odd, total in ((0, fe), (1, fo)):
            main = (
                total[rows64, 0:256]
                + le[rows64, 384 + 256 * odd : 640 + 256 * odd].astype(F32)
                + bt_ref[0:1, 0:256]
            )
            mine = pltpu.roll(tail, 64, 1) if odd else tail
            rim = total[rows64, 256:384] + jnp.where(keep, mine, 0.0) + bt_ref[0:1, 256:384]
            main = main.astype(BF)
            rim = rim.astype(BF)
            rows = pl.ds(pl.multiple_of(p * 128 + odd * 64, 64), 64)
            fr[rows, 0:256] = main
            fr[rows, 256:384] = rim
            main = main.astype(F32)
            rim = rim.astype(F32)
            mean = (
                jnp.sum(main[:, 0:128] + main[:, 128:256] + rim, axis=1, keepdims=True)
            ) * (1.0 / C)
            dm = main - mean
            dr = jnp.where(keep, rim - mean, 0.0)
            square = dm * dm
            var = jnp.sum(
                square[:, 0:128] + square[:, 128:256] + dr * dr, axis=1, keepdims=True
            ) * (1.0 / C)
            scale = lax.rsqrt(var + 1e-05)
            nm[rows, 0:256] = (
                dm * scale * gain_ref[0:1, 0:256] + bias_ref[0:1, 0:256]
            ).astype(BF)
            nm[rows, 256:384] = (
                dr * scale * gain_ref[0:1, 256:384] + bias_ref[0:1, 256:384]
            ).astype(BF)

    def norms(step, carry):
        for u in range(NORM_UNROLL):
            norm(step * NORM_UNROLL + u)
        return carry

    lax.fori_loop(0, GROUP // NORM_UNROLL, norms, 0)
    for half in range(2):
        rows = slice(half * 512, (half + 1) * 512)
        qkv[rows, :] = jnp.dot(nm[rows, :], wqkv_ref[...], preferred_element_type=F32).astype(BF)

    wide = lax.broadcasted_iota(jnp.int32, (128, 128), 1) < 64

    nt = (((1,), (1,)), ((), ()))

    ones = jnp.ones((128, 128), BF)

    def score(p):
        rows = pl.ds(pl.multiple_of(p * 128, 128), 128)
        for pair in range(2):
            q = qkv[rows, pair * 128 : (pair + 1) * 128]
            k = qkv[rows, 256 + pair * 128 : 384 + pair * 128]
            zero = jnp.zeros_like(q)
            both = jnp.concatenate([jnp.where(wide, q, zero), jnp.where(wide, zero, q)], axis=0)
            to = pl.ds(pl.multiple_of(p * 640 + pair * 256, 128), 256)
            sc[to, :] = lax.dot_general(both, k, nt, preferred_element_type=F32)
        to = pl.ds(pl.multiple_of(p * 640 + 512, 128), 128)
        sc[to, :] = lax.dot_general(
            qkv[rows, 768:896], qkv[rows, 896:1024], nt, preferred_element_type=F32
        )

    def raise_one(p):
        for at5 in range(5):
            rows = pl.ds(pl.multiple_of(p * 640 + at5 * 128, 128), 128)
            scores = sc[rows, :]
            top = jnp.max(scores, axis=1, keepdims=True)
            ex[rows, :] = jnp.exp2((scores - top) * EXP_SCALE).astype(BF)

    def gather(p):
        rows = pl.ds(pl.multiple_of(p * 128, 128), 128)
        for pair in range(2):
            v = qkv[rows, 512 + pair * 128 : 640 + pair * 128]
            to = pl.ds(pl.multiple_of(p * 640 + pair * 256, 128), 256)
            out = jnp.dot(
                ex[to, :], jnp.concatenate([v, ones], axis=1), preferred_element_type=F32
            )
            top = jnp.where(wide, out[0:128, 0:128], out[128:256, 0:128])
            under = jnp.where(wide, out[0:128, 128:256], out[128:256, 128:256])
            at[rows, pair * 128 : (pair + 1) * 128] = (top / under).astype(BF)
        to = pl.ds(pl.multiple_of(p * 640 + 512, 128), 128)
        qv = qkv[rows, 768:896]
        out = jnp.dot(ex[to, :], jnp.concatenate([qv, ones], axis=1), preferred_element_type=F32)
        at[rows, 256:384] = (out[:, 0:128] / out[:, 128:256]).astype(BF)

    def step(n, carry):
        for u in range(2):
            p = n * 2 + u
            gather(p - 2)
            raise_one(p - 1)
            score(p)
        return carry

    score(0)
    raise_one(0)
    score(1)
    lax.fori_loop(1, GROUP // 2, step, 0)
    gather(GROUP - 2)
    raise_one(GROUP - 1)
    gather(GROUP - 1)
    for half in range(2):
        rows = slice(half * 512, (half + 1) * 512)
        y = (
            fr[rows, :].astype(F32)
            + jnp.dot(at[rows, :], wout_ref[...], preferred_element_type=F32)
            + bout_ref[0:1, :]
        )
        for j in range(4):
            p = half * 4 + j
            even = y[j * 128 : j * 128 + 64]
            odd = y[j * 128 + 64 : j * 128 + 128]
            place = pl.ds(p, 64, stride=8)
            for c in range(2):
                ys[c, place, :] = even[:, c * 128 : (c + 1) * 128]
                ys[2 + c, place, :] = odd[:, c * 128 : (c + 1) * 128]
            ys[4, place, :] = jnp.where(keep, even[:, 256:384], pltpu.roll(odd[:, 256:384], 64, 1))
    for c in range(5):
        lanes = slice(c * 128, (c + 1) * 128)
        for j in range(0, 64, 2):
            two = [ys[c, n * 8 : n * 8 + 8, :] for n in ORDER[j : j + 2]]
            out_ref[j : j + 2, 0, :, lanes] = jnp.stack(two).astype(BF)


def attend_chunk(x, weights):
    count = x.shape[1]
    block = pl.BlockSpec((64, 1, 8, LANES), lambda i: (0, i, 0, 0))
    far = pl.BlockSpec(memory_space=pltpu.HBM)
    return pl.pallas_call(
        attend_kernel,
        out_shape=jax.ShapeDtypeStruct(x.shape, BF),
        grid=(count,),
        in_specs=[block, far, far, full(weights[2].shape), far, far],
        out_specs=block,
        scratch_shapes=[
            pltpu.VMEM((5, 512, 128), F32),
            pltpu.VMEM((512, 1024), BF),
            pltpu.VMEM((512, 1024), BF),
            pltpu.VMEM((512, CP), F32),
            pltpu.VMEM((512, CP), F32),
            pltpu.VMEM((1024, CP), BF),
            pltpu.VMEM((1024, CP), BF),
            pltpu.VMEM((1024, 1024), BF),
            pltpu.VMEM((1024, CP), BF),
            pltpu.VMEM((5, 512, 128), F32),
            pltpu.VMEM((5120, 128), F32),
            pltpu.VMEM((5120, 128), BF),
            pltpu.VMEM((1024, CP), BF),
            pltpu.VMEM((1024, CP), BF),
            pltpu.VMEM((CP, 1024), BF),
            pltpu.VMEM((CP, CP), BF),
            pltpu.SemaphoreType.DMA((4,)),
        ],
        compiler_params=pltpu.CompilerParams(vmem_limit_bytes=32 << 20),
        cost_estimate=pl.CostEstimate(
            flops=4000000000 * count, transcendentals=700000 * count, bytes_accessed=4000000 * count
        ),
        name="attend",
    )(x, *weights)


def final_kernel(x_ref, *rest):
    out = rest[-1]
    step = pl.program_id(0)
    for i in range(CHUNK):
        y = x_ref[i * 16 : (i + 1) * 16, step].reshape(128, LANES).T
        out[0, i, 0:256, :] = y[0:256]
        out[1, i, 0:256, :] = y[256:512]
        out[0, i, 256:320, :] = y[512:576]
        out[1, i, 256:320, :] = y[576:640]


def final_chunk(x, held, first, step, rows):
    count = x.shape[1]
    operands = [x]
    specs = [pl.BlockSpec(memory_space=pltpu.VMEM)]
    aliases = {}
    if held is not None:
        operands.append(held)
        specs.append(pl.BlockSpec(memory_space=pl.ANY))
        aliases = {1: 0}
    return pl.pallas_call(
        final_kernel,
        out_shape=jax.ShapeDtypeStruct((2, rows, C, 128), BF),
        grid=(count,),
        in_specs=specs,
        out_specs=pl.BlockSpec((2, CHUNK, C, 128), lambda i: (0, first + i * step, 0, 0)),
        input_output_aliases=aliases,
        compiler_params=pltpu.CompilerParams(vmem_limit_bytes=16 << 20),
        cost_estimate=pl.CostEstimate(
            flops=0, transcendentals=0, bytes_accessed=1400000 * count
        ),
        name="final",
    )(*operands)


def prepare_kernel(wt_ref, wq_ref, wk_ref, wv_ref, wo_ref, *outs):
    even, odd, qkv, mix = outs
    zero = jnp.zeros((64, CP), BF)
    side = jnp.zeros((C, 64), BF)
    wide = [jnp.concatenate([wt_ref[k], side], axis=1) for k in range(3)]
    a, b, c = 256, 320, 384
    for at, tap, low, high in (
        (0, 0, 0, a),
        (c - 64, 0, a, b),
        (c, 1, 0, a),
        (640, 2, 0, a),
        (896, 1, a, b),
        (960, 2, a, b),
    ):
        even[at : at + high - low, :] = wide[tap][low:high]
    even[a:b, :] = zero
    for at, tap, low, high in (
        (0, 0, 0, a),
        (a, 1, 0, a),
        (512, 0, a, b),
        (576, 1, a, b),
        (640, 2, 0, a),
        (896, 2, a, b),
    ):
        odd[at : at + high - low, :] = wide[tap][low:high]
    odd[960:1024, :] = zero
    qkv[C:CP, :] = jnp.zeros((64, 1024), BF)
    qkv[0:C, 0:256] = wq_ref[:, 0:256]
    qkv[0:C, 256:512] = wk_ref[:, 0:256]
    qkv[0:C, 512:768] = wv_ref[:, 0:256]
    qkv[0:C, 768:896] = jnp.concatenate([wq_ref[:, 256:C], wv_ref[:, 256:C]], axis=1)
    qkv[0:C, 896:1024] = jnp.concatenate([wk_ref[:, 256:C], side], axis=1)
    out = jnp.concatenate([wo_ref[...], side], axis=1)
    mix[0:256, :] = out[0:256]
    mix[256:320, :] = zero
    mix[320:384, :] = out[256:320]


def prepared(w_temporal, w_query, w_key, w_value, w_out):
    square = full((C, C))
    shapes = ((1024, CP), (1024, CP), (CP, 1024), (CP, CP))
    return pl.pallas_call(
        prepare_kernel,
        out_shape=[pltpu.HBM(shape, BF) for shape in shapes],
        grid=(1,),
        in_specs=[full((3, C, C)), square, square, square, square],
        out_specs=[full(shape) for shape in shapes],
        compiler_params=pltpu.CompilerParams(vmem_limit_bytes=16 << 20),
        cost_estimate=pl.CostEstimate(flops=0, transcendentals=0, bytes_accessed=5000000),
        name="prepare",
    )(w_temporal, w_query, w_key, w_value, w_out)


def on_device(
    clip,
    w_spatial,
    b_spatial,
    w_temporal,
    b_temporal,
    ln_gain,
    ln_bias,
    w_query,
    w_key,
    w_value,
    w_out,
    b_out,
):
    rows = clip.shape[1]
    x = jnp.transpose(clip, (0, 1, 3, 2))
    row_count = lax.axis_size("row")
    forward = [(i, i + 1) for i in range(row_count - 1)]
    backward = [(b, a) for a, b in forward]
    low = lax.ppermute(x[:, rows - 1 :], "row", forward)
    high = lax.ppermute(x[:, :1], "row", backward)
    x = pltpu.with_memory_space_constraint(x, pltpu.HBM)
    w_spatial = pltpu.with_memory_space_constraint(w_spatial, pltpu.HBM)
    bias = pltpu.with_memory_space_constraint(b_spatial, pltpu.HBM)
    w_even, w_odd, w_qkv, w_mix = prepared(w_temporal, w_query, w_key, w_value, w_out)
    vectors = jnp.pad(jnp.stack([b_temporal, ln_gain, ln_bias, b_out]), ((0, 4), (0, CP - C)))
    w_even, w_odd, w_qkv, w_mix = (
        pltpu.with_memory_space_constraint(w, pltpu.HBM) for w in (w_even, w_odd, w_qkv, w_mix)
    )
    weights = (w_even, w_odd, vectors, w_qkv, w_mix)

    def exchange(value):
        return lax.all_to_all(
            value,
            "frame",
            split_axis=0,
            concat_axis=0,
            tiled=True,
            axis_index_groups=[list(ORDER)],
        )

    held = None
    for parts in ((1,), (0, 2)):
        sent = spatial_chunk(parts, low, x, high, w_spatial, bias)
        sent = exchange(sent)
        sent = attend_chunk(sent, weights)
        sent = exchange(sent)
        held = final_chunk(sent, held, parts[0], parts[-1] - parts[0], rows)
    return jnp.transpose(held, (0, 1, 3, 2))


def solution(mesh):
    placed = (P("frame", "row", None, None),) + (P(),) * 11
    return jax.shard_map(
        on_device,
        mesh=mesh,
        in_specs=placed,
        out_specs=P("frame", "row", None, None),
        check_vma=False,
    )
```
